32 devices in a mesh: row: 2 (over y), col: 16 (over z, x, core).
Axes of the slice: x: 2, y: 2, z: 4, core: 2. Of those that a mesh axis runs over, the one named last changes fastest.
Arguments:
- blocks: bfloat16 [128, 2048, 128], P('row', 'col'), may hold values from -0.1875 to 0.1875
- block_rows: int32 [2, 1024], P('row', 'col'), may hold values from 0 to 2047, as said below
- block_cols: int32 [2, 1024], P('row', 'col'), may hold values from 0 to 255
- counts: int32 [2, 16], P('row', 'col'), may hold values from 1 to 64, as said below
- start_vectors: float32 [32, 524288], P(None, ('row', 'col')), may hold values from -6 to 6
Outputs:
- vectors: float32 [32, 524288], P(None, ('row', 'col'))
The draws below stay inside these ranges and needn't reach their ends.
Inputs may be any that keep to these rules, and one draw needn't show every extreme that they name: counts[r, c] is the number of live slots of grid position (r, c); in every draw some position has all 64 slots live. For every grid position (r, c) and every o < 16, exactly 4 of its 64 slots have block_rows[r, c * 64 + s] // 128 == o.
All inputs are finite; a program needn't handle non-finite values.
Results may differ from the reference program's by a relative error of at most 0.0036.
Values may be sent and summed in bfloat16 or wider, within the bound.
A program may use at most 256 MiB of HBM per device.

```python
import jax
import jax.numpy as jnp
from jax import lax

N = 524288
K = 32
BS = 128
SLOTS = 64
ITERS = 2
PB = 128
CB = 256
N_ROW = 2
N_COL = 16


def draw_counts(key, part):
    first_key = jax.random.fold_in(key, 11)
    second_key = jax.random.fold_in(key, 23)
    uniform_ints = jax.random.randint(first_key, (N_ROW * N_COL,), 1, SLOTS + 1)
    skewed = jnp.clip(uniform_ints * uniform_ints // SLOTS, 1, SLOTS)
    fullest = jax.random.randint(second_key, (), 0, N_ROW * N_COL)
    skewed = jnp.where(jnp.arange(N_ROW * N_COL) == fullest, SLOTS, skewed)
    return skewed.reshape(N_ROW, N_COL).astype(jnp.int32)


def draw_block_rows(key, part):
    order_key = jax.random.fold_in(key, 5)
    offset_key = jax.random.fold_in(key, 7)
    tile_total = N_ROW * N_COL
    owner_base = jnp.tile(jnp.arange(N_COL, dtype=jnp.int32), SLOTS // N_COL)
    tile_keys = jax.random.split(order_key, tile_total)
    owners = jax.vmap(lambda one_key: jax.random.permutation(one_key, owner_base))(tile_keys)
    offsets = jax.random.randint(offset_key, (tile_total, SLOTS), 0, PB)
    return (owners * PB + offsets).reshape(N_ROW, N_COL * SLOTS).astype(jnp.int32)


def set_ends(values, rng, smallest, high):
    place = [jax.random.randint(jax.random.fold_in(rng, axis), (), 0, length) for axis, length in enumerate(values.shape)]
    widest = values.shape.index(max(values.shape))
    next_to = place[:widest] + [(place[widest] + 1) % values.shape[widest]] + place[widest + 1:]
    return values.at[tuple(place)].set(smallest).at[tuple(next_to)].set(high)


def block_scale(own_key, extent, cuts, least, largest):
    factor_of = 1.0
    for axis_at, blocks in cuts:
        heights = jax.random.uniform(jax.random.fold_in(jax.random.fold_in(own_key, 6), axis_at), (blocks,), jnp.float32, least / len(cuts), largest / len(cuts))
        factor_of = factor_of * jnp.repeat(jnp.exp(heights), extent[axis_at] // blocks).reshape((-1,) + (1,) * (len(extent) - 1 - axis_at))
    return factor_of


def bell_draw(stream_key, dims, scale, bound, cuts=(), kind=jnp.bfloat16):
    result = scale * jax.random.normal(stream_key, dims, jnp.float32)
    if cuts:
        result = result * block_scale(stream_key, dims, cuts, -0.22, 0.18)
    return jnp.clip(result, -bound, bound).astype(kind)


def setup_inputs(seed: int = 0) -> dict:
    seeds = jax.random.split(jax.random.key(seed), 6)
    return {
        "blocks": bell_draw(seeds[0], (N_ROW * SLOTS, N_COL * BS, BS), (BS * 8) ** -0.5, 0.1875, ((0, 2), (1, 16))),
        "block_rows": draw_block_rows(jax.random.fold_in(seeds[5], 71), 0),
        "block_cols": set_ends(jax.random.randint(seeds[2], (N_ROW, N_COL * SLOTS), 0, CB), jax.random.fold_in(seeds[2], 1), 0, CB - 1).astype(jnp.int32),
        "counts": draw_counts(jax.random.fold_in(seeds[5], 71), 0),
        "start_vectors": bell_draw(seeds[4], (K, N), 1.0, 6.0, ((1, 32),), jnp.float32),
    }


def cholesky_lower(gram_matrix):
    matrix_order = gram_matrix.shape[0]
    positions = jnp.arange(matrix_order)

    def column_step(position, factor):
        before = (positions < position).astype(gram_matrix.dtype)
        target_row = lax.dynamic_index_in_dim(factor, position, 0, keepdims=False) * before
        column = lax.dynamic_index_in_dim(gram_matrix, position, 1, keepdims=False)
        residue = column - lax.optimization_barrier(jnp.sum(factor * target_row[None, :], axis=1))
        on_diagonal = positions == position
        pivot_value = jnp.sqrt(jnp.sum(jnp.where(on_diagonal, residue, 0.0)))
        values = jnp.where(on_diagonal, pivot_value, residue / pivot_value)
        values = jnp.where(positions >= position, values, 0.0)
        return lax.dynamic_update_index_in_dim(factor, values, position, 1)
    return lax.fori_loop(0, matrix_order, column_step, jnp.zeros_like(gram_matrix))

def lower_inverse(lower_factor):
    matrix_order = lower_factor.shape[0]
    positions = jnp.arange(matrix_order)

    def row_step(position, inverse):
        lower_row = lax.dynamic_index_in_dim(lower_factor, position, 0, keepdims=False)
        before = (positions < position).astype(lower_factor.dtype)
        inner_sum = lax.optimization_barrier(jnp.sum((lower_row * before)[:, None] * inverse, axis=0))
        unit_row = (positions == position).astype(lower_factor.dtype)
        pivot_value = jnp.sum(lower_row * unit_row)
        return lax.dynamic_update_index_in_dim(inverse, (unit_row - inner_sum) / pivot_value, position, 0)
    return lax.fori_loop(0, matrix_order, row_step, jnp.zeros_like(lower_factor))

def reference(blocks, block_rows, block_cols, counts, start_vectors):
    block_count = N // BS
    row_span = PB * N_COL
    slot_ids = jnp.arange(SLOTS, dtype=jnp.int32)
    tile_order = jnp.arange(N_ROW * N_COL, dtype=jnp.int32)
    vectors = start_vectors
    for iteration in range(ITERS):
        narrow = lax.optimization_barrier(vectors.astype(jnp.bfloat16))
        rounded = narrow.astype(jnp.float32).reshape(K, block_count, BS)

        def one_tile(image_rows, tile_index):
            grid_row = tile_index // N_COL
            grid_col = tile_index % N_COL
            tile_blocks = lax.dynamic_slice(blocks, (grid_row * SLOTS, grid_col * BS, jnp.int32(0)), (SLOTS, BS, BS)).astype(jnp.float32)
            local_rows = lax.dynamic_slice(block_rows, (grid_row, grid_col * SLOTS), (1, SLOTS))[0].astype(jnp.int32)
            local_cols = lax.dynamic_slice(block_cols, (grid_row, grid_col * SLOTS), (1, SLOTS))[0].astype(jnp.int32)
            live_count = lax.dynamic_slice(counts, (grid_row, grid_col), (1, 1))[0, 0]
            global_rows = grid_row * row_span + local_rows
            global_cols = local_cols // PB * row_span + grid_col * PB + local_cols % PB
            live_mask = (slot_ids < live_count).astype(jnp.float32)
            from_cols = jnp.take(rounded, global_cols, axis=1)
            from_rows = jnp.take(rounded, global_rows, axis=1)
            to_rows = jnp.einsum('kgj,gij->kgi', from_cols, tile_blocks, precision=lax.Precision.HIGHEST) * live_mask[None, :, None]
            to_cols = jnp.einsum('kgi,gij->kgj', from_rows, tile_blocks, precision=lax.Precision.HIGHEST) * live_mask[None, :, None]
            image_rows = image_rows.at[:, global_rows].add(to_rows)
            image_rows = image_rows.at[:, global_cols].add(to_cols)
            return (image_rows, None)
        image_rows = lax.scan(one_tile, jnp.zeros((K, block_count, BS), jnp.float32), tile_order)[0]
        product = image_rows.reshape(K, N)
        gram_matrix = jnp.dot(product, product.T, precision=lax.Precision.HIGHEST, preferred_element_type=jnp.float32) / N
        inverse = lower_inverse(cholesky_lower(gram_matrix))
        vectors = jnp.dot(inverse, product, precision=lax.Precision.HIGHEST, preferred_element_type=jnp.float32)
    return vectors
```

```python
import functools

import jax
import jax.numpy as jnp
from jax import lax
from jax.experimental import pallas as pl
from jax.experimental.pallas import tpu as pltpu
from jax.sharding import PartitionSpec as P

ITERS = 2
GROUPS = 4
LANES = 128
MESH = pl.DeviceIdType.MESH
ANY = pl.BlockSpec(memory_space=pl.ANY)
VMEM = pl.BlockSpec(memory_space=pltpu.VMEM)
SMEM = pl.BlockSpec(memory_space=pltpu.SMEM)
KERNEL_BYTES = 60 << 20
FINISH_BYTES = 48 << 20
NO_KEY = 1 << 20


def partner(me, d, size):
    other, w = 0, 1
    while w < size:
        step = d // w if isinstance(d, int) else lax.div(d, w)
        other = other + w * lax.rem(lax.div(me, w) + step, 2)
        w *= 2
    return other


def split(value):
    high = value.astype(jnp.bfloat16)
    return high, (value - high.astype(jnp.float32)).astype(jnp.bfloat16)


def inverse_stack(inverse):
    high, low = split(inverse)
    return jnp.concatenate([high, low, high, low], axis=1)


def pair(blocks, i):
    return jnp.concatenate([blocks[2 * i], blocks[2 * i + 1]], axis=1)


def apply_inverse(stacked, product):
    high, low = split(product)
    parts = jnp.concatenate([high, high, low, low], axis=0)
    return jnp.dot(stacked, parts, preferred_element_type=jnp.float32)


def factor_inverse(packed, size):
    full = jnp.concatenate([packed[:, size * i : size * (i + 1)] for i in range(size // 8)], axis=0)
    rows = lax.broadcasted_iota(jnp.int32, (size, size), 0)
    lanes = lax.broadcasted_iota(jnp.int32, (size, size), 1)
    work = jnp.concatenate([full, (rows == lanes).astype(jnp.float32)], axis=1)
    row_ids = lax.broadcasted_iota(jnp.int32, work.shape, 0)
    for j in range(size):
        column = jnp.broadcast_to(work[:, j : j + 1], work.shape)
        pivot_row = work[j : j + 1, :] * (1.0 / column[j : j + 1, :])
        work = work - jnp.where(row_ids > j, column, 0.0) * pivot_row
    pivots = jnp.sum(jnp.where(rows == lanes, work[:, :size], 0.0), axis=1, keepdims=True)
    return work[:, size:] * (1.0 / jnp.sqrt(pivots))


def gram_term(value):
    high, low = split(value)
    parts = jnp.concatenate([high, low], axis=0)
    return lax.dot_general(
        parts, parts, (((1,), (1,)), ((), ())), preferred_element_type=jnp.float32
    )


def pack_gram(total, vectors):
    upper = total[:vectors] + total[vectors:]
    full = upper[:, :vectors] + upper[:, vectors:]
    return jnp.concatenate([full[8 * i : 8 * i + 8] for i in range(vectors // 8)], axis=1)


def iota(shape, axis):
    return lax.broadcasted_iota(jnp.int32, shape, axis)


def column(row):
    n = row.shape[1]
    return jnp.sum(jnp.where(iota((n, n), 0) == iota((n, n), 1), row, 0), axis=1, keepdims=True)


def step_kernel(
    n_row,
    n_col,
    panel,
    order,
    block_rows,
    block_cols,
    counts,
    blocks,
    source,
    product_out,
    inverse_out,
    source_in,
    held,
    held_blocks,
    c_out,
    c_in,
    c_back,
    r_out,
    r_in,
    terms,
    runs,
    product,
    ask,
    mine,
    lists_v,
    asked_v,
    sort_v,
    stack,
    gram,
    gram_row,
    gram_sum,
    gram_col,
    mine_s,
    lists,
    asked,
    sort_s,
    own,
    l_send,
    l_recv,
    a_send,
    a_recv,
    c_send,
    c_recv,
    cb_send,
    cb_recv,
    r_send,
    r_recv,
    rb_send,
    rb_recv,
    gr_send,
    gr_recv,
    gc_send,
    gc_recv,
):
    slots, size = held_blocks.shape[0], held_blocks.shape[1]
    vectors = held.shape[1]
    share = slots // n_col
    per = n_col // GROUPS
    piece = per * share
    my_row, my_col = lax.axis_index("row"), lax.axis_index("col")
    base = my_row * panel
    f32, bf16 = jnp.float32, jnp.bfloat16

    load_source = pltpu.make_async_copy(source, source_in, own.at[0])
    load_blocks = pltpu.make_async_copy(blocks, held_blocks, own.at[1])
    load_source.start()
    load_blocks.start()

    def col_peer(d):
        return partner(my_col, d, n_col)

    def row_peer(e):
        return partner(my_row, e, n_row)

    def remote(src, dst, send, recv, row, col):
        return pltpu.make_async_remote_copy(
            src_ref=src,
            dst_ref=dst,
            send_sem=send,
            recv_sem=recv,
            device_id=(row, col),
            device_id_type=MESH,
        )

    barrier = pltpu.get_barrier_semaphore()
    for d in range(1, n_col):
        pl.semaphore_signal(barrier, inc=1, device_id=(my_row, col_peer(d)), device_id_type=MESH)
    for e in range(1, n_row):
        pl.semaphore_signal(barrier, inc=1, device_id=(row_peer(e), my_col), device_id_type=MESH)

    rows = block_rows[...]
    shift = panel.bit_length() - 1
    owner = lax.shift_right_logical(rows, shift)
    owner_c = column(owner)
    before = iota((slots, slots), 0) < iota((slots, slots), 1)
    rank = jnp.sum(jnp.where((owner_c == owner) & before, 1, 0), axis=0, keepdims=True)
    rank_c = column(rank)
    place_c = owner_c * share + rank_c
    ids = iota((slots, 1), 0)
    live = ids < counts[0, 0]
    row_c = jnp.where(live, column(rows & (panel - 1)) + 1, 0)
    col_c = jnp.where(live, column(block_cols[...]) + 1, 0)
    lanes = iota((slots, LANES), 1)
    here = place_c == lanes
    mine[0] = jnp.sum(jnp.where(here, ids, 0), axis=0, keepdims=True)
    mine[1] = jnp.sum(jnp.where(here, col_c, 0), axis=0, keepdims=True)
    mine_place = rank_c == lanes - my_col * share
    for o in range(n_col):
        ask[o] = jnp.sum(
            jnp.where(mine_place & (owner_c == o), row_c, 0), axis=0, keepdims=True
        )
    own_lists = [
        pltpu.make_async_copy(mine, mine_s, own.at[2]),
        pltpu.make_async_copy(ask.at[my_col], lists_v.at[my_col], own.at[3]),
        pltpu.make_async_copy(mine.at[1], asked_v.at[my_row], own.at[4]),
    ]
    for copy in own_lists:
        copy.start()

    load_source.wait()
    for b in range(panel):
        held[b] = source_in[:, b * size : (b + 1) * size].astype(bf16)

    pl.semaphore_wait(barrier, n_col + n_row - 2)

    row_asks = [
        remote(mine.at[1], asked_v.at[my_row], a_send.at[e], a_recv.at[e], row_peer(e), my_col)
        for e in range(1, n_row)
    ]
    for copy in row_asks:
        copy.start()

    def col_ask(d):
        q = col_peer(d)
        return remote(ask.at[q], lists_v.at[my_col], l_send.at[d], l_recv.at[d], my_row, q)

    for d in reversed(range(1, n_col)):
        col_ask(d).start()
    for copy in own_lists:
        copy.wait()
    for copy in row_asks:
        copy.wait()
    take_asked = pltpu.make_async_copy(asked_v, asked, own.at[4])
    take_asked.start()
    for d in reversed(range(1, n_col)):
        col_ask(d).wait()
    take_lists = pltpu.make_async_copy(lists_v, lists, own.at[3])
    take_lists.start()
    take_asked.wait()
    take_lists.wait()

    def first_slot(g):
        return partner(lax.div(my_col, per), g, GROUPS) * piece

    def row_copy(g, e):
        at = pl.ds(first_slot(g), piece)
        p = row_peer(e)
        return remote(
            r_out.at[e, at], r_in.at[e, at], r_send.at[e, g], r_recv.at[e, g], p, my_col
        )

    def row_back(g, e):
        at = pl.ds(slots + my_row * slots + first_slot(g), piece)
        p = row_peer(e)
        return remote(
            terms.at[at], terms.at[at], rb_send.at[e, g], rb_recv.at[e, g], p, my_col
        )

    def col_copy(d):
        return remote(
            c_out.at[d], c_in.at[d], c_send.at[d], c_recv.at[d], my_row, col_peer(d)
        )

    def col_back(d):
        at = pl.ds(my_col * share, share)
        return remote(
            c_back.at[d], terms.at[at], cb_send.at[d], cb_recv.at[d], my_row, col_peer(d)
        )

    def gather():
        for g in reversed(range(GROUPS)):
            for e in range(1, n_row):
                p, start = row_peer(e), first_slot(g)

                def one_r(n, carry):
                    at = asked[p, 0, start + n] - 1 - base
                    r_out[e, start + n] = held[jnp.clip(at, 0, panel - 1)]
                    return carry

                lax.fori_loop(0, piece, one_r, 0, unroll=8)
                row_copy(g, e).start()

            def one_c(i, carry):
                d = (g + 1) * per - 1 - i
                q = col_peer(d)

                def fill(target):
                    for a in range(share):
                        at = jnp.maximum(lists[q, 0, q * share + a] - 1, 0)
                        target[d, a] = held[at]

                fill(c_out)
                col_copy(d).start()
                return carry

            lax.fori_loop(0, per if g else per - 1, one_c, 0)
        for a in range(share):
            at = jnp.maximum(lists[my_col, 0, my_col * share + a] - 1, 0)
            c_in[0, a] = held[at]

    def multiply():
        for g in reversed(range(GROUPS)):
            for e in range(1, n_row):
                row_copy(g, e).wait()

            def one_peer(i, carry, own_terms=False):
                d = (g + 1) * per - 1 - i
                q = my_col if own_terms else col_peer(d)
                if not own_terms:
                    col_copy(d).wait()
                for a in range(share):
                    t = q * share + a
                    block = held_blocks[mine_s[0, 0, t]]
                    col = mine_s[1, 0, t] - 1
                    x_col = held[jnp.clip(col - base, 0, panel - 1)]
                    for e in range(1, n_row):
                        first_col = row_peer(e) * panel
                        there = (col >= first_col) & (col < first_col + panel)
                        x_col = jnp.where(there, r_in[e, t], x_col)
                    row_product = lax.dot_general(
                        x_col, block, (((1,), (1,)), ((), ())), preferred_element_type=f32
                    )
                    col_product = jnp.dot(c_in[d, a], block, preferred_element_type=f32)
                    if own_terms:
                        terms[t] = row_product.astype(bf16)
                    else:
                        c_back[d, a] = row_product.astype(bf16)
                    terms[slots + my_row * slots + t] = col_product.astype(bf16)
                if not own_terms:
                    col_back(d).start()
                return carry

            lax.fori_loop(0, per if g else per - 1, one_peer, 0)
            if g == 0:
                one_peer(per - 1, 0, own_terms=True)
            for e in range(1, n_row):
                row_back(g, e).start()

    def wait_terms():
        for g in reversed(range(GROUPS)):
            for e in range(1, n_row):
                row_back(g, e).wait()

        def one(i, carry):
            col_back(n_col - 1 - i).wait()
            return carry

        lax.fori_loop(0, n_col - 1, one, 0)

    term_count = slots * (n_row + 1)
    sort_rows = -(-term_count // LANES)

    def sort_terms():
        key_parts = []
        found = jnp.sum(lists_v[...], axis=0)
        key_parts.append(jnp.where(found > 0, found - 1, NO_KEY)[:, :slots])
        for p in range(n_row):
            at = asked_v[p] - 1 - base
            key_parts.append(jnp.where((at >= 0) & (at < panel), at, NO_KEY)[:, :slots])
        tail = sort_rows * LANES - term_count
        if tail:
            key_parts.append(jnp.full((1, tail), NO_KEY, jnp.int32))
        key = jnp.concatenate(key_parts, axis=1)
        total = sort_rows * LANES
        key_c = column(key)
        ids_c, ids_r = iota((total, total), 0), iota((total, total), 1)
        twin = (key_c == key) & (ids_c < ids_r)
        rank = jnp.sum(jnp.where(twin | (key_c < key), 1, 0), axis=0, keepdims=True)
        again = jnp.sum(jnp.where(twin, 1, 0), axis=0, keepdims=True)
        here = column(rank) == ids_r
        by_place = jnp.sum(jnp.where(here, ids_c, 0), axis=0, keepdims=True)
        goes_on = jnp.sum(jnp.where(here, column(again), 0), axis=0, keepdims=True)
        for i in range(sort_rows):
            sort_v[i] = by_place[:, i * LANES : (i + 1) * LANES]
            sort_v[sort_rows + i] = goes_on[:, i * LANES : (i + 1) * LANES]
        target = iota((total, LANES), 1)
        up_to = jnp.sum(jnp.where(key_c <= target, 1, 0), axis=0, keepdims=True)
        at_it = jnp.sum(jnp.where(key_c == target, 1, 0), axis=0, keepdims=True)
        sort_v[2 * sort_rows] = jnp.where(at_it > 0, up_to, 0)

    def add_terms():
        run = jnp.zeros((vectors, size), f32)
        for i in range(sort_rows):
            count = min(LANES, term_count - i * LANES)

            def one(n, run):
                term = terms[sort_s[i, 0, n]].astype(f32)
                run = jnp.where(sort_s[sort_rows + i, 0, n] > 0, run + term, term)
                runs[i * LANES + n] = run
                return run

            run = lax.fori_loop(0, count, one, run, unroll=8)

    def total_of(b):
        last = sort_s[2 * sort_rows, 0, b]
        return jnp.where(last > 0, runs[jnp.maximum(last - 1, 0)], 0.0)

    def gram_rows(i, e):
        p = row_peer(e)
        return remote(
            gram.at[i], gram_row.at[i, my_row], gr_send.at[i, e], gr_recv.at[i, e], p, my_col
        )

    def gram_cols(i, d):
        return remote(
            gram_sum.at[i],
            gram_col.at[i, my_col],
            gc_send.at[i, d],
            gc_recv.at[i, d],
            my_row,
            col_peer(d),
        )

    def send_gram(i, total):
        packed = pack_gram(total, vectors)
        gram[i] = packed
        for e in range(1, n_row):
            gram_rows(i, e).start()
        gram_row[i, my_row] = packed

    def pass_gram(i):
        for e in range(1, n_row):
            gram_rows(i, e).wait()
        partial = jnp.sum(gram_row[i], axis=0)
        gram_sum[i] = partial
        for d in reversed(range(1, n_col)):
            gram_cols(i, d).start()
        gram_col[i, my_col] = partial

    def take_gram(i):
        for d in range(1, n_col):
            gram_cols(i, d).wait()
        return factor_inverse(jnp.sum(gram_col[i], axis=0) / order, vectors)

    no_gram = jnp.zeros((2 * vectors, 2 * vectors), f32)

    gather()
    sort_terms()
    copy_sort = pltpu.make_async_copy(sort_v, sort_s, own.at[4])
    copy_sort.start()
    load_blocks.wait()
    multiply()
    copy_sort.wait()
    wait_terms()
    add_terms()

    def take_first(b, carry):
        total = total_of(b)
        product[b] = total
        held[b] = total.astype(bf16)
        return carry

    lax.fori_loop(0, panel, take_first, 0, unroll=8)

    gather()
    total = lax.fori_loop(
        0, panel // 2, lambda i, total: total + gram_term(pair(product, i)), no_gram, unroll=8
    )
    send_gram(0, total)
    pass_gram(0)
    multiply()
    stack[...] = inverse_stack(take_gram(0))
    wait_terms()
    add_terms()
    stacked = stack[...]

    def take_second(i, total):
        both = jnp.concatenate([total_of(2 * i), total_of(2 * i + 1)], axis=1)
        both = apply_inverse(stacked, both)
        product[2 * i] = both[:, :size]
        product[2 * i + 1] = both[:, size:]
        return total + gram_term(both)

    total = lax.fori_loop(0, panel // 2, take_second, no_gram, unroll=8)
    send_gram(1, total)
    store = pltpu.make_async_copy(product, product_out, own.at[0])
    store.start()
    pass_gram(1)
    inverse_out[...] = take_gram(1)
    store.wait()


def finish_kernel(source, inverse, out):
    stacked = inverse_stack(inverse[...])
    for i in range(source.shape[0] // 2):
        out[:, i * 256 : (i + 1) * 256] = apply_inverse(stacked, pair(source, i))


def per_device(n_row, n_col, blocks, block_rows, block_cols, counts, start_vectors):
    slots, size = blocks.shape[0], blocks.shape[1]
    vectors, width = start_vectors.shape
    panel = width // size
    share = slots // n_col
    f32, bf16, i32 = jnp.float32, jnp.bfloat16, jnp.int32
    shape = jax.ShapeDtypeStruct
    dma = pltpu.SemaphoreType.DMA
    gram_shape = (8, vectors * vectors // 8)
    order = float(n_row * n_col * width)
    terms = slots * (n_row + 1)
    sort_shape = (2 * (-(-terms // LANES)) + 1, 1, LANES)
    by_owner = (n_col, share, vectors, size)
    product, inverse = pl.pallas_call(
        functools.partial(step_kernel, n_row, n_col, panel, order),
        out_shape=(shape((panel, vectors, size), f32), shape((vectors, vectors), f32)),
        in_specs=[VMEM, VMEM, SMEM, ANY, ANY],
        out_specs=(ANY, VMEM),
        scratch_shapes=[
            pltpu.VMEM((vectors, width), f32),
            pltpu.VMEM((panel, vectors, size), bf16),
            pltpu.VMEM(blocks.shape, bf16),
            pltpu.VMEM(by_owner, bf16),
            pltpu.VMEM(by_owner, bf16),
            pltpu.VMEM(by_owner, bf16),
            pltpu.VMEM((n_row, slots, vectors, size), bf16),
            pltpu.VMEM((n_row, slots, vectors, size), bf16),
            pltpu.VMEM((terms, vectors, size), bf16),
            pltpu.VMEM((terms, vectors, size), f32),
            pltpu.VMEM((panel, vectors, size), f32),
            pltpu.VMEM((n_col, 1, LANES), i32),
            pltpu.VMEM((2, 1, LANES), i32),
            pltpu.VMEM((n_col, 1, LANES), i32),
            pltpu.VMEM((n_row, 1, LANES), i32),
            pltpu.VMEM(sort_shape, i32),
            pltpu.VMEM((vectors, 4 * vectors), bf16),
            pltpu.VMEM((2,) + gram_shape, f32),
            pltpu.VMEM((2, n_row) + gram_shape, f32),
            pltpu.VMEM((2,) + gram_shape, f32),
            pltpu.VMEM((2, n_col) + gram_shape, f32),
            pltpu.SMEM((2, 1, LANES), i32),
            pltpu.SMEM((n_col, 1, LANES), i32),
            pltpu.SMEM((n_row, 1, LANES), i32),
            pltpu.SMEM(sort_shape, i32),
            dma((5,)),
            dma((n_col,)),
            dma((n_col,)),
            dma((n_row,)),
            dma((n_row,)),
            dma((n_col,)),
            dma((n_col,)),
            dma((n_col,)),
            dma((n_col,)),
            dma((n_row, GROUPS)),
            dma((n_row, GROUPS)),
            dma((n_row, GROUPS)),
            dma((n_row, GROUPS)),
            dma((2, n_row)),
            dma((2, n_row)),
            dma((2, n_col)),
            dma((2, n_col)),
        ],
        compiler_params=pltpu.CompilerParams(
            collective_id=1, has_side_effects=True, vmem_limit_bytes=KERNEL_BYTES
        ),
    )(block_rows, block_cols, counts, blocks, start_vectors)
    return pl.pallas_call(
        finish_kernel,
        out_shape=shape((vectors, width), f32),
        in_specs=[VMEM, VMEM],
        out_specs=VMEM,
        compiler_params=pltpu.CompilerParams(vmem_limit_bytes=FINISH_BYTES),
    )(product, inverse)


def solution(mesh):
    placed = (
        P("row", "col", None),
        P("row", "col"),
        P("row", "col"),
        P("row", "col"),
        P(None, ("row", "col")),
    )
    return jax.shard_map(
        functools.partial(per_device, mesh.shape["row"], mesh.shape["col"]),
        mesh=mesh,
        in_specs=placed,
        out_specs=P(None, ("row", "col")),
        check_vma=False,
    )
```

```python
import functools

import jax
import jax.numpy as jnp
from jax import lax
from jax.experimental import pallas as pl
from jax.experimental.pallas import tpu as pltpu
from jax.sharding import PartitionSpec as P

ITERS = 2
GROUPS = 4
LANES = 128
MESH = pl.DeviceIdType.MESH
ANY = pl.BlockSpec(memory_space=pl.ANY)
KERNEL_BYTES = 60 << 20
NO_KEY = 1 << 20


def partner(me, d, size):
    other, w = 0, 1
    while w < size:
        step = d // w if isinstance(d, int) else lax.div(d, w)
        other = other + w * lax.rem(lax.div(me, w) + step, 2)
        w *= 2
    return other


def split(value):
    high = value.astype(jnp.bfloat16)
    return high, (value - high.astype(jnp.float32)).astype(jnp.bfloat16)


def inverse_stack(inverse):
    high, low = split(inverse)
    return jnp.concatenate([high, low, high, low], axis=1)


def pair(blocks, i):
    return jnp.concatenate([blocks[2 * i], blocks[2 * i + 1]], axis=1)


def apply_inverse(stacked, product):
    high, low = split(product)
    parts = jnp.concatenate([high, high, low, low], axis=0)
    return jnp.dot(stacked, parts, preferred_element_type=jnp.float32)


def factor_inverse(packed, size):
    full = jnp.concatenate([packed[:, size * i : size * (i + 1)] for i in range(size // 8)], axis=0)
    rows = lax.broadcasted_iota(jnp.int32, (size, size), 0)
    lanes = lax.broadcasted_iota(jnp.int32, (size, size), 1)
    work = jnp.concatenate([full, (rows == lanes).astype(jnp.float32)], axis=1)
    row_ids = lax.broadcasted_iota(jnp.int32, work.shape, 0)
    for j in range(size):
        column = jnp.broadcast_to(work[:, j : j + 1], work.shape)
        pivot_row = work[j : j + 1, :] * (1.0 / column[j : j + 1, :])
        work = work - jnp.where(row_ids > j, column, 0.0) * pivot_row
    pivots = jnp.sum(jnp.where(rows == lanes, work[:, :size], 0.0), axis=1, keepdims=True)
    return work[:, size:] * (1.0 / jnp.sqrt(pivots))


def gram_term(value):
    high, low = split(value)
    parts = jnp.concatenate([high, low], axis=0)
    return lax.dot_general(
        parts, parts, (((1,), (1,)), ((), ())), preferred_element_type=jnp.float32
    )


def pack_gram(total, vectors):
    upper = total[:vectors] + total[vectors:]
    full = upper[:, :vectors] + upper[:, vectors:]
    return jnp.concatenate([full[8 * i : 8 * i + 8] for i in range(vectors // 8)], axis=1)


def iota(shape, axis):
    return lax.broadcasted_iota(jnp.int32, shape, axis)


def column(row):
    n = row.shape[1]
    return jnp.sum(jnp.where(iota((n, n), 0) == iota((n, n), 1), row, 0), axis=1, keepdims=True)


def step_kernel(
    n_row,
    n_col,
    panel,
    order,
    rows_in,
    cols_in,
    counts_in,
    blocks,
    source,
    product_out,
    inverse_out,
    block_rows,
    block_cols,
    counts,
    source_in,
    held,
    held_blocks,
    c_out,
    c_in,
    c_back,
    r_out,
    r_in,
    terms,
    runs,
    product,
    ask,
    mine,
    lists_v,
    asked_v,
    sort_v,
    stack,
    inverse,
    gram,
    gram_row,
    gram_sum,
    gram_col,
    mine_s,
    lists,
    asked,
    sort_s,
    own,
    l_send,
    l_recv,
    a_send,
    a_recv,
    c_send,
    c_recv,
    cb_send,
    cb_recv,
    r_send,
    r_recv,
    rb_send,
    rb_recv,
    gr_send,
    gr_recv,
    gc_send,
    gc_recv,
):
    slots, size = held_blocks.shape[0], held_blocks.shape[1]
    vectors = held.shape[1]
    share = slots // n_col
    per = n_col // GROUPS
    piece = per * share
    my_row, my_col = lax.axis_index("row"), lax.axis_index("col")
    base = my_row * panel
    f32, bf16 = jnp.float32, jnp.bfloat16

    load_source = pltpu.make_async_copy(source, source_in, own.at[0])
    load_blocks = pltpu.make_async_copy(blocks, held_blocks, own.at[1])
    load_slots = [
        pltpu.make_async_copy(rows_in, block_rows, own.at[2]),
        pltpu.make_async_copy(cols_in, block_cols, own.at[3]),
        pltpu.make_async_copy(counts_in, counts, own.at[4]),
    ]
    for copy in load_slots:
        copy.start()
    load_source.start()
    load_blocks.start()

    def col_peer(d):
        return partner(my_col, d, n_col)

    def row_peer(e):
        return partner(my_row, e, n_row)

    def remote(src, dst, send, recv, row, col):
        return pltpu.make_async_remote_copy(
            src_ref=src,
            dst_ref=dst,
            send_sem=send,
            recv_sem=recv,
            device_id=(row, col),
            device_id_type=MESH,
        )

    barrier = pltpu.get_barrier_semaphore()
    for d in range(1, n_col):
        pl.semaphore_signal(barrier, inc=1, device_id=(my_row, col_peer(d)), device_id_type=MESH)
    for e in range(1, n_row):
        pl.semaphore_signal(barrier, inc=1, device_id=(row_peer(e), my_col), device_id_type=MESH)

    for copy in load_slots:
        copy.wait()

    rows = block_rows[...]
    shift = panel.bit_length() - 1
    owner = lax.shift_right_logical(rows, shift)
    owner_c = column(owner)
    before = iota((slots, slots), 0) < iota((slots, slots), 1)
    rank = jnp.sum(jnp.where((owner_c == owner) & before, 1, 0), axis=0, keepdims=True)
    rank_c = column(rank)
    place_c = owner_c * share + rank_c
    ids = iota((slots, 1), 0)
    live = ids < counts[0, 0]
    row_c = jnp.where(live, column(rows & (panel - 1)) + 1, 0)
    col_c = jnp.where(live, column(block_cols[...]) + 1, 0)
    lanes = iota((slots, LANES), 1)
    here = place_c == lanes
    mine[0] = jnp.sum(jnp.where(here, ids, 0), axis=0, keepdims=True)
    mine[1] = jnp.sum(jnp.where(here, col_c, 0), axis=0, keepdims=True)
    mine_place = rank_c == lanes - my_col * share
    for o in range(n_col):
        ask[o] = jnp.sum(
            jnp.where(mine_place & (owner_c == o), row_c, 0), axis=0, keepdims=True
        )
    take_mine = pltpu.make_async_copy(mine, mine_s, own.at[2])
    take_mine.start()
    lists_v[my_col] = ask[my_col]
    asked_v[my_row] = mine[1]

    load_source.wait()
    for b in range(panel):
        held[b] = source_in[:, b * size : (b + 1) * size].astype(bf16)

    pl.semaphore_wait(barrier, n_col + n_row - 2)

    def row_ask(e):
        p = row_peer(e)
        return remote(
            mine.at[1], asked_v.at[my_row], a_send.at[e], a_recv.at[e], p, my_col
        )

    def col_ask(d):
        q = col_peer(d)
        return remote(
            ask.at[q], lists_v.at[my_col], l_send.at[d], l_recv.at[d], my_row, q
        )

    def first_peer(g):
        return partner(lax.div(my_col, per), g, GROUPS) * per

    def take_lists(g):
        at = pl.ds(first_peer(g), per)
        return pltpu.make_async_copy(lists_v.at[at], lists.at[at], own.at[5 + g])

    take_asked = pltpu.make_async_copy(asked_v, asked, own.at[4])
    for e in range(1, n_row):
        row_ask(e).start()
    for d in reversed(range(1, n_col)):
        col_ask(d).start()
    take_mine.wait()
    for e in range(1, n_row):
        row_ask(e).wait()
    take_asked.start()
    take_asked.wait()

    def first_slot(g):
        return first_peer(g) * share

    def row_copy(g, e):
        at = pl.ds(first_slot(g), piece)
        p = row_peer(e)
        return remote(
            r_out.at[e, at], r_in.at[e, at], r_send.at[e, g], r_recv.at[e, g], p, my_col
        )

    def row_back(g, e):
        at = pl.ds(slots + my_row * slots + first_slot(g), piece)
        p = row_peer(e)
        return remote(
            terms.at[at], terms.at[at], rb_send.at[e, g], rb_recv.at[e, g], p, my_col
        )

    def col_copy(d):
        return remote(
            c_out.at[d], c_in.at[d], c_send.at[d], c_recv.at[d], my_row, col_peer(d)
        )

    def col_back(d):
        at = pl.ds(my_col * share, share)
        return remote(
            c_back.at[d], terms.at[at], cb_send.at[d], cb_recv.at[d], my_row, col_peer(d)
        )

    def gather(first):
        def block(at):
            if first:
                return held[at]
            return total_of(at).astype(bf16)

        for g in reversed(range(GROUPS)):
            for e in range(1, n_row):
                p, start = row_peer(e), first_slot(g)

                def one_r(n, carry):
                    at = asked[p, 0, start + n] - 1 - base
                    r_out[e, start + n] = block(jnp.clip(at, 0, panel - 1))
                    return carry

                lax.fori_loop(0, piece, one_r, 0, unroll=8)
                row_copy(g, e).start()
        for g in reversed(range(GROUPS)):
            if first:
                for d in reversed(range(max(g * per, 1), (g + 1) * per)):
                    col_ask(d).wait()
                take_lists(g).start()
                take_lists(g).wait()

            def one_c(i, carry):
                d = (g + 1) * per - 1 - i
                q = col_peer(d)
                for a in range(share):
                    at = jnp.maximum(lists[q, 0, q * share + a] - 1, 0)
                    c_out[d, a] = block(at)
                col_copy(d).start()
                return carry

            lax.fori_loop(0, per if g else per - 1, one_c, 0)
        for a in range(share):
            at = jnp.maximum(lists[my_col, 0, my_col * share + a] - 1, 0)
            c_in[0, a] = block(at)

    def multiply():
        for g in reversed(range(GROUPS)):
            for e in range(1, n_row):
                row_copy(g, e).wait()

            def one_peer(i, carry, own_terms=False):
                d = (g + 1) * per - 1 - i
                q = my_col if own_terms else col_peer(d)
                if not own_terms:
                    col_copy(d).wait()
                for a in range(share):
                    t = q * share + a
                    block = held_blocks[mine_s[0, 0, t]]
                    col = mine_s[1, 0, t] - 1
                    x_col = held[jnp.clip(col - base, 0, panel - 1)]
                    for e in range(1, n_row):
                        first_col = row_peer(e) * panel
                        there = (col >= first_col) & (col < first_col + panel)
                        x_col = jnp.where(there, r_in[e, t], x_col)
                    row_product = lax.dot_general(
                        x_col, block, (((1,), (1,)), ((), ())), preferred_element_type=f32
                    )
                    col_product = jnp.dot(c_in[d, a], block, preferred_element_type=f32)
                    if own_terms:
                        terms[t] = row_product.astype(bf16)
                    else:
                        c_back[d, a] = row_product.astype(bf16)
                    terms[slots + my_row * slots + t] = col_product.astype(bf16)
                if not own_terms:
                    col_back(d).start()
                return carry

            lax.fori_loop(0, per if g else per - 1, one_peer, 0)
            if g == 0:
                one_peer(per - 1, 0, own_terms=True)
            for e in range(1, n_row):
                row_back(g, e).start()

    def wait_terms():
        for g in reversed(range(GROUPS)):
            for e in range(1, n_row):
                row_back(g, e).wait()

        def one(i, carry):
            col_back(n_col - 1 - i).wait()
            return carry

        lax.fori_loop(0, n_col - 1, one, 0)

    term_count = slots * (n_row + 1)
    sort_rows = -(-term_count // LANES)

    def sort_terms():
        key_parts = []
        found = jnp.sum(lists_v[...], axis=0)
        key_parts.append(jnp.where(found > 0, found - 1, NO_KEY)[:, :slots])
        for p in range(n_row):
            at = asked_v[p] - 1 - base
            key_parts.append(jnp.where((at >= 0) & (at < panel), at, NO_KEY)[:, :slots])
        tail = sort_rows * LANES - term_count
        if tail:
            key_parts.append(jnp.full((1, tail), NO_KEY, jnp.int32))
        key = jnp.concatenate(key_parts, axis=1)
        total = sort_rows * LANES
        key_c = column(key)
        ids_c, ids_r = iota((total, total), 0), iota((total, total), 1)
        twin = (key_c == key) & (ids_c < ids_r)
        rank = jnp.sum(jnp.where(twin | (key_c < key), 1, 0), axis=0, keepdims=True)
        again = jnp.sum(jnp.where(twin, 1, 0), axis=0, keepdims=True)
        here = column(rank) == ids_r
        by_place = jnp.sum(jnp.where(here, ids_c, 0), axis=0, keepdims=True)
        goes_on = jnp.sum(jnp.where(here, column(again), 0), axis=0, keepdims=True)
        for i in range(sort_rows):
            sort_v[i] = by_place[:, i * LANES : (i + 1) * LANES]
            sort_v[sort_rows + i] = goes_on[:, i * LANES : (i + 1) * LANES]
        target = iota((total, LANES), 1)
        up_to = jnp.sum(jnp.where(key_c <= target, 1, 0), axis=0, keepdims=True)
        at_it = jnp.sum(jnp.where(key_c == target, 1, 0), axis=0, keepdims=True)
        sort_v[2 * sort_rows] = jnp.where(at_it > 0, up_to, 0)

    def add_terms():
        run = jnp.zeros((vectors, size), f32)
        for i in range(sort_rows):
            count = min(LANES, term_count - i * LANES)

            def one(n, run):
                term = terms[sort_s[i, 0, n]].astype(f32)
                run = jnp.where(sort_s[sort_rows + i, 0, n] > 0, run + term, term)
                runs[i * LANES + n] = run
                return run

            run = lax.fori_loop(0, count, one, run, unroll=8)

    def total_of(b):
        last = sort_s[2 * sort_rows, 0, b]
        return jnp.where(last > 0, runs[jnp.maximum(last - 1, 0)], 0.0)

    def gram_rows(i, e):
        p = row_peer(e)
        return remote(
            gram.at[i], gram_row.at[i, my_row], gr_send.at[i, e], gr_recv.at[i, e], p, my_col
        )

    def gram_cols(i, d):
        return remote(
            gram_sum.at[i],
            gram_col.at[i, my_col],
            gc_send.at[i, d],
            gc_recv.at[i, d],
            my_row,
            col_peer(d),
        )

    def send_gram(i, total):
        packed = pack_gram(total, vectors)
        gram[i] = packed
        for e in range(1, n_row):
            gram_rows(i, e).start()
        gram_row[i, my_row] = packed

    def pass_gram(i):
        for e in range(1, n_row):
            gram_rows(i, e).wait()
        partial = jnp.sum(gram_row[i], axis=0)
        gram_sum[i] = partial
        for d in reversed(range(1, n_col)):
            gram_cols(i, d).start()
        gram_col[i, my_col] = partial

    def take_gram(i):
        for d in range(1, n_col):
            gram_cols(i, d).wait()
        return factor_inverse(jnp.sum(gram_col[i], axis=0) / order, vectors)

    no_gram = jnp.zeros((2 * vectors, 2 * vectors), f32)

    gather(True)
    sort_terms()
    copy_sort = pltpu.make_async_copy(sort_v, sort_s, own.at[4])
    copy_sort.start()
    load_blocks.wait()
    multiply()
    copy_sort.wait()
    wait_terms()
    add_terms()

    gather(False)

    def take_first(i, total):
        both = jnp.concatenate([total_of(2 * i), total_of(2 * i + 1)], axis=1)
        held[2 * i] = both[:, :size].astype(bf16)
        held[2 * i + 1] = both[:, size:].astype(bf16)
        return total + gram_term(both)

    total = lax.fori_loop(0, panel // 2, take_first, no_gram, unroll=8)
    send_gram(0, total)
    pass_gram(0)
    multiply()
    stack[...] = inverse_stack(take_gram(0))
    wait_terms()
    add_terms()
    stacked = stack[...]

    def take_second(i, total):
        both = jnp.concatenate([total_of(2 * i), total_of(2 * i + 1)], axis=1)
        both = apply_inverse(stacked, both)
        product[2 * i] = both[:, :size]
        product[2 * i + 1] = both[:, size:]
        return total + gram_term(both)

    total = lax.fori_loop(0, panel // 2, take_second, no_gram, unroll=8)
    send_gram(1, total)
    store = pltpu.make_async_copy(product, product_out, own.at[0])
    store.start()
    pass_gram(1)
    inverse[...] = take_gram(1)
    store_inverse = pltpu.make_async_copy(inverse, inverse_out, own.at[1])
    store_inverse.start()
    store.wait()
    store_inverse.wait()


def finish_kernel(chunks, source, inverse_in, out, held, inverse, done, in_sems, out_sems):
    load_inverse = pltpu.make_async_copy(inverse_in, inverse, in_sems.at[chunks])
    load_inverse.start()
    panel, wide = held.shape[0] // chunks, out.shape[1] // chunks

    def load(j):
        at = pl.ds(j * panel, panel)
        return pltpu.make_async_copy(source.at[at], held.at[at], in_sems.at[j])

    def store(j):
        at = pl.ds(j * wide, wide)
        return pltpu.make_async_copy(done.at[:, at], out.at[:, at], out_sems.at[j])

    for j in range(chunks):
        load(j).start()
    load_inverse.wait()
    stacked = inverse_stack(inverse[...])
    for j in range(chunks):
        load(j).wait()
        for i in range(j * panel // 2, (j + 1) * panel // 2):
            done[:, i * 256 : (i + 1) * 256] = apply_inverse(stacked, pair(held, i))
        store(j).start()
    for j in range(chunks):
        store(j).wait()


def per_device(n_row, n_col, blocks, block_rows, block_cols, counts, start_vectors):
    slots, size = blocks.shape[0], blocks.shape[1]
    vectors, width = start_vectors.shape
    panel = width // size
    share = slots // n_col
    f32, bf16, i32 = jnp.float32, jnp.bfloat16, jnp.int32
    shape = jax.ShapeDtypeStruct
    dma = pltpu.SemaphoreType.DMA
    gram_shape = (8, vectors * vectors // 8)
    order = float(n_row * n_col * width)
    terms = slots * (n_row + 1)
    sort_shape = (2 * (-(-terms // LANES)) + 1, 1, LANES)
    by_owner = (n_col, share, vectors, size)
    product, inverse = pl.pallas_call(
        functools.partial(step_kernel, n_row, n_col, panel, order),
        out_shape=(shape((panel, vectors, size), f32), shape((vectors, vectors), f32)),
        in_specs=[ANY] * 5,
        out_specs=(ANY, ANY),
        scratch_shapes=[
            pltpu.VMEM(block_rows.shape, i32),
            pltpu.VMEM(block_cols.shape, i32),
            pltpu.SMEM(counts.shape, i32),
            pltpu.VMEM((vectors, width), f32),
            pltpu.VMEM((panel, vectors, size), bf16),
            pltpu.VMEM(blocks.shape, bf16),
            pltpu.VMEM(by_owner, bf16),
            pltpu.VMEM(by_owner, bf16),
            pltpu.VMEM(by_owner, bf16),
            pltpu.VMEM((n_row, slots, vectors, size), bf16),
            pltpu.VMEM((n_row, slots, vectors, size), bf16),
            pltpu.VMEM((terms, vectors, size), bf16),
            pltpu.VMEM((terms, vectors, size), f32),
            pltpu.VMEM((panel, vectors, size), f32),
            pltpu.VMEM((n_col, 1, LANES), i32),
            pltpu.VMEM((2, 1, LANES), i32),
            pltpu.VMEM((n_col, 1, LANES), i32),
            pltpu.VMEM((n_row, 1, LANES), i32),
            pltpu.VMEM(sort_shape, i32),
            pltpu.VMEM((vectors, 4 * vectors), bf16),
            pltpu.VMEM((vectors, vectors), f32),
            pltpu.VMEM((2,) + gram_shape, f32),
            pltpu.VMEM((2, n_row) + gram_shape, f32),
            pltpu.VMEM((2,) + gram_shape, f32),
            pltpu.VMEM((2, n_col) + gram_shape, f32),
            pltpu.SMEM((2, 1, LANES), i32),
            pltpu.SMEM((n_col, 1, LANES), i32),
            pltpu.SMEM((n_row, 1, LANES), i32),
            pltpu.SMEM(sort_shape, i32),
            dma((5 + GROUPS,)),
            dma((n_col,)),
            dma((n_col,)),
            dma((n_row,)),
            dma((n_row,)),
            dma((n_col,)),
            dma((n_col,)),
            dma((n_col,)),
            dma((n_col,)),
            dma((n_row, GROUPS)),
            dma((n_row, GROUPS)),
            dma((n_row, GROUPS)),
            dma((n_row, GROUPS)),
            dma((2, n_row)),
            dma((2, n_row)),
            dma((2, n_col)),
            dma((2, n_col)),
        ],
        compiler_params=pltpu.CompilerParams(
            collective_id=1, has_side_effects=True, vmem_limit_bytes=KERNEL_BYTES
        ),
    )(block_rows, block_cols, counts, blocks, start_vectors)
    chunks = min(8, panel // 2)
    return pl.pallas_call(
        functools.partial(finish_kernel, chunks),
        out_shape=shape((vectors, width), f32),
        in_specs=[ANY, ANY],
        out_specs=ANY,
        scratch_shapes=[
            pltpu.VMEM((panel, vectors, size), f32),
            pltpu.VMEM((vectors, vectors), f32),
            pltpu.VMEM((vectors, width), f32),
            dma((chunks + 1,)),
            dma((chunks,)),
        ],
        compiler_params=pltpu.CompilerParams(vmem_limit_bytes=KERNEL_BYTES),
    )(product, inverse)


def solution(mesh):
    placed = (
        P("row", "col", None),
        P("row", "col"),
        P("row", "col"),
        P("row", "col"),
        P(None, ("row", "col")),
    )
    return jax.shard_map(
        functools.partial(per_device, mesh.shape["row"], mesh.shape["col"]),
        mesh=mesh,
        in_specs=placed,
        out_specs=P(None, ("row", "col")),
        check_vma=False,
    )
```

```python
import functools

import jax
import jax.numpy as jnp
from jax import lax
from jax.experimental import pallas as pl
from jax.experimental.pallas import tpu as pltpu
from jax.sharding import PartitionSpec as P

ITERS = 2
GROUPS = 4
LANES = 128
MESH = pl.DeviceIdType.MESH
ANY = pl.BlockSpec(memory_space=pl.ANY)
KERNEL_BYTES = 60 << 20
NO_KEY = 1 << 20


def partner(me, d, size):
    other, w = 0, 1
    while w < size:
        step = d // w if isinstance(d, int) else lax.div(d, w)
        other = other + w * lax.rem(lax.div(me, w) + step, 2)
        w *= 2
    return other


def split(value):
    high = value.astype(jnp.bfloat16)
    return high, (value - high.astype(jnp.float32)).astype(jnp.bfloat16)


def inverse_stack(inverse):
    high, low = split(inverse)
    return jnp.concatenate([high, low, high, low], axis=1)


def pair(blocks, i):
    return jnp.concatenate([blocks[2 * i], blocks[2 * i + 1]], axis=1)


def apply_inverse(stacked, product):
    high, low = split(product)
    parts = jnp.concatenate([high, high, low, low], axis=0)
    return jnp.dot(stacked, parts, preferred_element_type=jnp.float32)


def factor_inverse(packed, size):
    full = jnp.concatenate([packed[:, size * i : size * (i + 1)] for i in range(size // 8)], axis=0)
    rows = lax.broadcasted_iota(jnp.int32, (size, size), 0)
    lanes = lax.broadcasted_iota(jnp.int32, (size, size), 1)
    work = jnp.concatenate([full, (rows == lanes).astype(jnp.float32)], axis=1)
    row_ids = lax.broadcasted_iota(jnp.int32, work.shape, 0)
    for j in range(0, size, 8):
        columns = [jnp.broadcast_to(work[:, j + k : j + k + 1], work.shape) for k in range(8)]
        pivot_rows = [work[j + k : j + k + 1, :] for k in range(8)]
        for k in range(8):
            at = j + k
            scale = 1.0 / columns[k][at : at + 1, :]
            pivot_row = pivot_rows[k] * scale
            for m in range(k + 1, 8):
                factor = columns[m][at : at + 1, :] * scale
                pivot_rows[m] = pivot_rows[m] - columns[k][j + m : j + m + 1, :] * pivot_row
                columns[m] = columns[m] - columns[k] * factor
            work = work - jnp.where(row_ids > at, columns[k], 0.0) * pivot_row
    pivots = jnp.sum(jnp.where(rows == lanes, work[:, :size], 0.0), axis=1, keepdims=True)
    return work[:, size:] * (1.0 / jnp.sqrt(pivots))


def gram_term(value):
    high, low = split(value)
    parts = jnp.concatenate([high, low], axis=0)
    return lax.dot_general(
        parts, parts, (((1,), (1,)), ((), ())), preferred_element_type=jnp.float32
    )


def pack_gram(total, vectors):
    upper = total[:vectors] + total[vectors:]
    full = upper[:, :vectors] + upper[:, vectors:]
    return jnp.concatenate([full[8 * i : 8 * i + 8] for i in range(vectors // 8)], axis=1)


def iota(shape, axis):
    return lax.broadcasted_iota(jnp.int32, shape, axis)


def column(row):
    n = row.shape[1]
    return jnp.sum(jnp.where(iota((n, n), 0) == iota((n, n), 1), row, 0), axis=1, keepdims=True)


def step_kernel(
    n_row,
    n_col,
    panel,
    order,
    rows_in,
    cols_in,
    counts_in,
    blocks,
    source,
    product_out,
    inverse_out,
    block_rows,
    block_cols,
    counts,
    source_in,
    held,
    held_blocks,
    c_out,
    c_in,
    c_back,
    r_out,
    r_in,
    terms,
    runs,
    product,
    ask,
    mine,
    lists_v,
    asked_v,
    sort_v,
    stack,
    inverse,
    gram,
    gram_row,
    gram_col,
    gram_all,
    mine_s,
    lists,
    asked,
    sort_s,
    own,
    l_send,
    l_recv,
    a_send,
    a_recv,
    c_send,
    c_recv,
    cb_send,
    cb_recv,
    r_send,
    r_recv,
    rb_send,
    rb_recv,
    gr_send,
    gr_recv,
    gc_send,
    gc_recv,
    g_send,
    g_recv,
):
    slots, size = held_blocks.shape[0], held_blocks.shape[1]
    vectors = held.shape[1]
    share = slots // n_col
    per = n_col // GROUPS
    piece = per * share
    my_row, my_col = lax.axis_index("row"), lax.axis_index("col")
    base = my_row * panel
    f32, bf16 = jnp.float32, jnp.bfloat16

    load_source = pltpu.make_async_copy(source, source_in, own.at[0])
    load_blocks = pltpu.make_async_copy(blocks, held_blocks, own.at[1])
    load_slots = [
        pltpu.make_async_copy(rows_in, block_rows, own.at[2]),
        pltpu.make_async_copy(cols_in, block_cols, own.at[3]),
        pltpu.make_async_copy(counts_in, counts, own.at[4]),
    ]
    for copy in load_slots:
        copy.start()
    load_source.start()
    load_blocks.start()

    def col_peer(d):
        return partner(my_col, d, n_col)

    def row_peer(e):
        return partner(my_row, e, n_row)

    def remote(src, dst, send, recv, row, col):
        return pltpu.make_async_remote_copy(
            src_ref=src,
            dst_ref=dst,
            send_sem=send,
            recv_sem=recv,
            device_id=(row, col),
            device_id_type=MESH,
        )

    barrier = pltpu.get_barrier_semaphore()
    for d in range(1, n_col):
        pl.semaphore_signal(barrier, inc=1, device_id=(my_row, col_peer(d)), device_id_type=MESH)
    for e in range(1, n_row):
        pl.semaphore_signal(barrier, inc=1, device_id=(row_peer(e), my_col), device_id_type=MESH)

    for copy in load_slots:
        copy.wait()

    rows = block_rows[...]
    shift = panel.bit_length() - 1
    owner = lax.shift_right_logical(rows, shift)
    owner_c = column(owner)
    before = iota((slots, slots), 0) < iota((slots, slots), 1)
    rank = jnp.sum(jnp.where((owner_c == owner) & before, 1, 0), axis=0, keepdims=True)
    rank_c = column(rank)
    place_c = owner_c * share + rank_c
    ids = iota((slots, 1), 0)
    live = ids < counts[0, 0]
    row_c = jnp.where(live, column(rows & (panel - 1)) + 1, 0)
    col_c = jnp.where(live, column(block_cols[...]) + 1, 0)
    lanes = iota((slots, LANES), 1)
    here = place_c == lanes
    mine[0] = jnp.sum(jnp.where(here, ids, 0), axis=0, keepdims=True)
    mine[1] = jnp.sum(jnp.where(here, col_c, 0), axis=0, keepdims=True)
    mine_place = rank_c == lanes - my_col * share
    for o in range(n_col):
        ask[o] = jnp.sum(
            jnp.where(mine_place & (owner_c == o), row_c, 0), axis=0, keepdims=True
        )
    take_mine = pltpu.make_async_copy(mine, mine_s, own.at[2])
    take_mine.start()
    lists_v[my_col] = ask[my_col]
    asked_v[my_row] = mine[1]

    load_source.wait()
    for b in range(panel):
        held[b] = source_in[:, b * size : (b + 1) * size].astype(bf16)

    pl.semaphore_wait(barrier, n_col + n_row - 2)

    def row_ask(e):
        p = row_peer(e)
        return remote(
            mine.at[1], asked_v.at[my_row], a_send.at[e], a_recv.at[e], p, my_col
        )

    def col_ask(d):
        q = col_peer(d)
        return remote(
            ask.at[q], lists_v.at[my_col], l_send.at[d], l_recv.at[d], my_row, q
        )

    def first_peer(g):
        return partner(lax.div(my_col, per), g, GROUPS) * per

    def take_lists(g):
        at = pl.ds(first_peer(g), per)
        return pltpu.make_async_copy(lists_v.at[at], lists.at[at], own.at[5 + g])

    take_asked = pltpu.make_async_copy(asked_v, asked, own.at[4])
    for e in range(1, n_row):
        row_ask(e).start()
    for d in reversed(range(1, n_col)):
        col_ask(d).start()
    take_mine.wait()
    for e in range(1, n_row):
        row_ask(e).wait()
    take_asked.start()
    take_asked.wait()

    def first_slot(g):
        return first_peer(g) * share

    def row_copy(g, e):
        at = pl.ds(first_slot(g), piece)
        p = row_peer(e)
        return remote(
            r_out.at[e, at], r_in.at[e, at], r_send.at[e, g], r_recv.at[e, g], p, my_col
        )

    def row_back(g, e):
        at = pl.ds(slots + my_row * slots + first_slot(g), piece)
        p = row_peer(e)
        return remote(
            terms.at[at], terms.at[at], rb_send.at[e, g], rb_recv.at[e, g], p, my_col
        )

    def col_copy(d):
        return remote(
            c_out.at[d], c_in.at[d], c_send.at[d], c_recv.at[d], my_row, col_peer(d)
        )

    def col_back(d):
        at = pl.ds(my_col * share, share)
        return remote(
            c_back.at[d], terms.at[at], cb_send.at[d], cb_recv.at[d], my_row, col_peer(d)
        )

    def gather(first):
        def block(at):
            if first:
                return held[at]
            return total_of(at).astype(bf16)

        for g in reversed(range(GROUPS)):
            for e in range(1, n_row):
                p, start = row_peer(e), first_slot(g)

                def one_r(n, carry):
                    at = asked[p, 0, start + n] - 1 - base
                    r_out[e, start + n] = block(jnp.clip(at, 0, panel - 1))
                    return carry

                lax.fori_loop(0, piece, one_r, 0, unroll=8)
                row_copy(g, e).start()
        for g in reversed(range(GROUPS)):
            if first:
                for d in reversed(range(max(g * per, 1), (g + 1) * per)):
                    col_ask(d).wait()
                take_lists(g).start()
                take_lists(g).wait()

            def one_c(i, carry):
                d = (g + 1) * per - 1 - i
                q = col_peer(d)
                for a in range(share):
                    at = jnp.maximum(lists[q, 0, q * share + a] - 1, 0)
                    c_out[d, a] = block(at)
                col_copy(d).start()
                return carry

            lax.fori_loop(0, per if g else per - 1, one_c, 0)
        for a in range(share):
            at = jnp.maximum(lists[my_col, 0, my_col * share + a] - 1, 0)
            c_in[0, a] = block(at)

    def multiply(between=None):
        for g in reversed(range(GROUPS)):
            if between is not None and g == GROUPS - 2:
                between()
            for e in range(1, n_row):
                row_copy(g, e).wait()

            def one_peer(i, carry, own_terms=False):
                d = (g + 1) * per - 1 - i
                q = my_col if own_terms else col_peer(d)
                if not own_terms:
                    col_copy(d).wait()
                for a in range(share):
                    t = q * share + a
                    block = held_blocks[mine_s[0, 0, t]]
                    col = mine_s[1, 0, t] - 1
                    x_col = held[jnp.clip(col - base, 0, panel - 1)]
                    for e in range(1, n_row):
                        first_col = row_peer(e) * panel
                        there = (col >= first_col) & (col < first_col + panel)
                        x_col = jnp.where(there, r_in[e, t], x_col)
                    row_product = lax.dot_general(
                        x_col, block, (((1,), (1,)), ((), ())), preferred_element_type=f32
                    )
                    col_product = jnp.dot(c_in[d, a], block, preferred_element_type=f32)
                    if own_terms:
                        terms[t] = row_product.astype(bf16)
                    else:
                        c_back[d, a] = row_product.astype(bf16)
                    terms[slots + my_row * slots + t] = col_product.astype(bf16)
                if not own_terms:
                    col_back(d).start()
                return carry

            lax.fori_loop(0, per if g else per - 1, one_peer, 0)
            if g == 0:
                one_peer(per - 1, 0, own_terms=True)
            for e in range(1, n_row):
                row_back(g, e).start()

    def wait_terms():
        for g in reversed(range(GROUPS)):
            for e in range(1, n_row):
                row_back(g, e).wait()

        def one(i, carry):
            col_back(n_col - 1 - i).wait()
            return carry

        lax.fori_loop(0, n_col - 1, one, 0)

    term_count = slots * (n_row + 1)
    sort_rows = -(-term_count // LANES)

    def sort_terms():
        key_parts = []
        found = jnp.sum(lists_v[...], axis=0)
        key_parts.append(jnp.where(found > 0, found - 1, NO_KEY)[:, :slots])
        for p in range(n_row):
            at = asked_v[p] - 1 - base
            key_parts.append(jnp.where((at >= 0) & (at < panel), at, NO_KEY)[:, :slots])
        tail = sort_rows * LANES - term_count
        if tail:
            key_parts.append(jnp.full((1, tail), NO_KEY, jnp.int32))
        key = jnp.concatenate(key_parts, axis=1)
        total = sort_rows * LANES
        key_c = column(key)
        ids_c, ids_r = iota((total, total), 0), iota((total, total), 1)
        twin = (key_c == key) & (ids_c < ids_r)
        rank = jnp.sum(jnp.where(twin | (key_c < key), 1, 0), axis=0, keepdims=True)
        again = jnp.sum(jnp.where(twin, 1, 0), axis=0, keepdims=True)
        here = column(rank) == ids_r
        by_place = jnp.sum(jnp.where(here, ids_c, 0), axis=0, keepdims=True)
        goes_on = jnp.sum(jnp.where(here, column(again), 0), axis=0, keepdims=True)
        for i in range(sort_rows):
            sort_v[i] = by_place[:, i * LANES : (i + 1) * LANES]
            sort_v[sort_rows + i] = goes_on[:, i * LANES : (i + 1) * LANES]
        target = iota((total, LANES), 1)
        up_to = jnp.sum(jnp.where(key_c <= target, 1, 0), axis=0, keepdims=True)
        at_it = jnp.sum(jnp.where(key_c == target, 1, 0), axis=0, keepdims=True)
        sort_v[2 * sort_rows] = jnp.where(at_it > 0, up_to, 0)

    def add_terms():
        run = jnp.zeros((vectors, size), f32)
        for i in range(sort_rows):
            count = min(LANES, term_count - i * LANES)

            def one(n, run):
                term = terms[sort_s[i, 0, n]].astype(f32)
                run = jnp.where(sort_s[sort_rows + i, 0, n] > 0, run + term, term)
                runs[i * LANES + n] = run
                return run

            run = lax.fori_loop(0, count, one, run, unroll=8)

    def total_of(b):
        last = sort_s[2 * sort_rows, 0, b]
        return jnp.where(last > 0, runs[jnp.maximum(last - 1, 0)], 0.0)

    def gram_rows(e):
        p = row_peer(e)
        return remote(
            gram.at[0], gram_row.at[my_row], gr_send.at[e], gr_recv.at[e], p, my_col
        )

    def gram_cols(d):
        q = col_peer(d)
        return remote(
            gram.at[1], gram_col.at[my_col], gc_send.at[d], gc_recv.at[d], my_row, q
        )

    me = my_row * n_col + my_col

    def gram_copy(e, d):
        at = e * n_col + d
        p, q = row_peer(e), col_peer(d)
        return remote(gram.at[2], gram_all.at[me], g_send.at[at], g_recv.at[at], p, q)

    def send_first(total):
        packed = pack_gram(total, vectors)
        gram[0] = packed
        for e in range(1, n_row):
            gram_rows(e).start()
        gram_row[my_row] = packed

    def pass_first():
        for e in range(1, n_row):
            gram_rows(e).wait()
        partial = jnp.sum(gram_row[...], axis=0)
        gram[1] = partial
        for d in reversed(range(1, n_col)):
            gram_cols(d).start()
        gram_col[my_col] = partial

    def take_first_sum():
        for d in range(1, n_col):
            gram_cols(d).wait()
        return jnp.sum(gram_col[...], axis=0) / order

    others = [(e, d) for e in range(n_row) for d in range(n_col) if e or d][::-1]

    def sum_second(total):
        packed = pack_gram(total, vectors)
        gram[2] = packed
        for e, d in others:
            gram_copy(e, d).start()
        gram_all[me] = packed
        store.start()
        for e, d in others:
            gram_copy(e, d).wait()
        return jnp.sum(gram_all[...], axis=0) / order

    no_gram = jnp.zeros((2 * vectors, 2 * vectors), f32)

    gather(True)
    sort_terms()
    copy_sort = pltpu.make_async_copy(sort_v, sort_s, own.at[4])
    copy_sort.start()
    load_blocks.wait()
    multiply()
    copy_sort.wait()
    wait_terms()
    add_terms()

    gather(False)

    def take_first(i, total):
        both = jnp.concatenate([total_of(2 * i), total_of(2 * i + 1)], axis=1)
        held[2 * i] = both[:, :size].astype(bf16)
        held[2 * i + 1] = both[:, size:].astype(bf16)
        return total + gram_term(both)

    total = lax.fori_loop(0, panel // 2, take_first, no_gram, unroll=8)
    send_first(total)
    multiply(pass_first)
    stack[...] = inverse_stack(factor_inverse(take_first_sum(), vectors))
    wait_terms()
    add_terms()
    stacked = stack[...]

    def take_second(i, total):
        both = jnp.concatenate([total_of(2 * i), total_of(2 * i + 1)], axis=1)
        both = apply_inverse(stacked, both)
        product[2 * i] = both[:, :size]
        product[2 * i + 1] = both[:, size:]
        return total + gram_term(both)

    total = lax.fori_loop(0, panel // 2, take_second, no_gram, unroll=8)
    store = pltpu.make_async_copy(product, product_out, own.at[0])
    inverse[...] = factor_inverse(sum_second(total), vectors)
    store_inverse = pltpu.make_async_copy(inverse, inverse_out, own.at[1])
    store_inverse.start()
    store.wait()
    store_inverse.wait()


def finish_kernel(chunks, source, inverse_in, out, held, inverse, done, in_sems, out_sems):
    load_inverse = pltpu.make_async_copy(inverse_in, inverse, in_sems.at[chunks])
    load_inverse.start()
    panel, wide = held.shape[0] // chunks, out.shape[1] // chunks

    def load(j):
        at = pl.ds(j * panel, panel)
        return pltpu.make_async_copy(source.at[at], held.at[at], in_sems.at[j])

    def store(j):
        at = pl.ds(j * wide, wide)
        return pltpu.make_async_copy(done.at[:, at], out.at[:, at], out_sems.at[j])

    for j in range(chunks):
        load(j).start()
    load_inverse.wait()
    stacked = inverse_stack(inverse[...])
    for j in range(chunks):
        load(j).wait()
        for i in range(j * panel // 2, (j + 1) * panel // 2):
            done[:, i * 256 : (i + 1) * 256] = apply_inverse(stacked, pair(held, i))
        store(j).start()
    for j in range(chunks):
        store(j).wait()


def per_device(n_row, n_col, blocks, block_rows, block_cols, counts, start_vectors):
    slots, size = blocks.shape[0], blocks.shape[1]
    vectors, width = start_vectors.shape
    panel = width // size
    share = slots // n_col
    f32, bf16, i32 = jnp.float32, jnp.bfloat16, jnp.int32
    shape = jax.ShapeDtypeStruct
    dma = pltpu.SemaphoreType.DMA
    gram_shape = (8, vectors * vectors // 8)
    order = float(n_row * n_col * width)
    terms = slots * (n_row + 1)
    sort_shape = (2 * (-(-terms // LANES)) + 1, 1, LANES)
    by_owner = (n_col, share, vectors, size)
    product, inverse = pl.pallas_call(
        functools.partial(step_kernel, n_row, n_col, panel, order),
        out_shape=(shape((panel, vectors, size), f32), shape((vectors, vectors), f32)),
        in_specs=[ANY] * 5,
        out_specs=(ANY, ANY),
        scratch_shapes=[
            pltpu.VMEM(block_rows.shape, i32),
            pltpu.VMEM(block_cols.shape, i32),
            pltpu.SMEM(counts.shape, i32),
            pltpu.VMEM((vectors, width), f32),
            pltpu.VMEM((panel, vectors, size), bf16),
            pltpu.VMEM(blocks.shape, bf16),
            pltpu.VMEM(by_owner, bf16),
            pltpu.VMEM(by_owner, bf16),
            pltpu.VMEM(by_owner, bf16),
            pltpu.VMEM((n_row, slots, vectors, size), bf16),
            pltpu.VMEM((n_row, slots, vectors, size), bf16),
            pltpu.VMEM((terms, vectors, size), bf16),
            pltpu.VMEM((terms, vectors, size), f32),
            pltpu.VMEM((panel, vectors, size), f32),
            pltpu.VMEM((n_col, 1, LANES), i32),
            pltpu.VMEM((2, 1, LANES), i32),
            pltpu.VMEM((n_col, 1, LANES), i32),
            pltpu.VMEM((n_row, 1, LANES), i32),
            pltpu.VMEM(sort_shape, i32),
            pltpu.VMEM((vectors, 4 * vectors), bf16),
            pltpu.VMEM((vectors, vectors), f32),
            pltpu.VMEM((3,) + gram_shape, f32),
            pltpu.VMEM((n_row,) + gram_shape, f32),
            pltpu.VMEM((n_col,) + gram_shape, f32),
            pltpu.VMEM((n_row * n_col,) + gram_shape, f32),
            pltpu.SMEM((2, 1, LANES), i32),
            pltpu.SMEM((n_col, 1, LANES), i32),
            pltpu.SMEM((n_row, 1, LANES), i32),
            pltpu.SMEM(sort_shape, i32),
            dma((5 + GROUPS,)),
            dma((n_col,)),
            dma((n_col,)),
            dma((n_row,)),
            dma((n_row,)),
            dma((n_col,)),
            dma((n_col,)),
            dma((n_col,)),
            dma((n_col,)),
            dma((n_row, GROUPS)),
            dma((n_row, GROUPS)),
            dma((n_row, GROUPS)),
            dma((n_row, GROUPS)),
            dma((n_row,)),
            dma((n_row,)),
            dma((n_col,)),
            dma((n_col,)),
            dma((n_row * n_col,)),
            dma((n_row * n_col,)),
        ],
        compiler_params=pltpu.CompilerParams(
            collective_id=1, has_side_effects=True, vmem_limit_bytes=KERNEL_BYTES
        ),
    )(block_rows, block_cols, counts, blocks, start_vectors)
    chunks = min(8, panel // 2)
    return pl.pallas_call(
        functools.partial(finish_kernel, chunks),
        out_shape=shape((vectors, width), f32),
        in_specs=[ANY, ANY],
        out_specs=ANY,
        scratch_shapes=[
            pltpu.VMEM((panel, vectors, size), f32),
            pltpu.VMEM((vectors, vectors), f32),
            pltpu.VMEM((vectors, width), f32),
            dma((chunks + 1,)),
            dma((chunks,)),
        ],
        compiler_params=pltpu.CompilerParams(vmem_limit_bytes=KERNEL_BYTES),
    )(product, inverse)


def solution(mesh):
    placed = (
        P("row", "col", None),
        P("row", "col"),
        P("row", "col"),
        P("row", "col"),
        P(None, ("row", "col")),
    )
    return jax.shard_map(
        functools.partial(per_device, mesh.shape["row"], mesh.shape["col"]),
        mesh=mesh,
        in_specs=placed,
        out_specs=P(None, ("row", "col")),
        check_vma=False,
    )
```

```python
import functools

import jax
import jax.numpy as jnp
from jax import lax
from jax.experimental import pallas as pl
from jax.experimental.pallas import tpu as pltpu
from jax.sharding import PartitionSpec as P

ITERS = 2
GROUPS = 4
ORDER = (3, 1, 2, 0)
LANES = 128
MESH = pl.DeviceIdType.MESH
ANY = pl.BlockSpec(memory_space=pl.ANY)
VMEM = pl.BlockSpec(memory_space=pltpu.VMEM)
SMEM = pl.BlockSpec(memory_space=pltpu.SMEM)
KERNEL_BYTES = 50 << 20
NO_KEY = 1 << 20


def partner(me, d, size):
    other, w = 0, 1
    while w < size:
        step = d // w if isinstance(d, int) else lax.div(d, w)
        other = other + w * lax.rem(lax.div(me, w) + step, 2)
        w *= 2
    return other


def split(value):
    high = value.astype(jnp.bfloat16)
    return high, (value - high.astype(jnp.float32)).astype(jnp.bfloat16)


def inverse_stack(inverse):
    high, low = split(inverse)
    return jnp.concatenate([high, low, high, low], axis=1)


def pair(blocks, i):
    return jnp.concatenate([blocks[2 * i], blocks[2 * i + 1]], axis=1)


def apply_inverse(stacked, product):
    high, low = split(product)
    parts = jnp.concatenate([high, high, low, low], axis=0)
    return jnp.dot(stacked, parts, preferred_element_type=jnp.float32)


def factor_inverse(packed, size):
    full = jnp.concatenate([packed[:, size * i : size * (i + 1)] for i in range(size // 8)], axis=0)
    rows = lax.broadcasted_iota(jnp.int32, (size, size), 0)
    lanes = lax.broadcasted_iota(jnp.int32, (size, size), 1)
    work = jnp.concatenate([full, (rows == lanes).astype(jnp.float32)], axis=1)
    row_ids = lax.broadcasted_iota(jnp.int32, work.shape, 0)
    for j in range(0, size, 8):
        columns = [jnp.broadcast_to(work[:, j + k : j + k + 1], work.shape) for k in range(8)]
        pivot_rows = [work[j + k : j + k + 1, :] for k in range(8)]
        for k in range(8):
            at = j + k
            scale = 1.0 / columns[k][at : at + 1, :]
            pivot_row = pivot_rows[k] * scale
            for m in range(k + 1, 8):
                factor = columns[m][at : at + 1, :] * scale
                pivot_rows[m] = pivot_rows[m] - columns[k][j + m : j + m + 1, :] * pivot_row
                columns[m] = columns[m] - columns[k] * factor
            work = work - jnp.where(row_ids > at, columns[k], 0.0) * pivot_row
    pivots = jnp.sum(jnp.where(rows == lanes, work[:, :size], 0.0), axis=1, keepdims=True)
    return work[:, size:] * (1.0 / jnp.sqrt(pivots))


def gram_term(value):
    high, low = split(value)
    parts = jnp.concatenate([high, low], axis=0)
    return lax.dot_general(
        parts, parts, (((1,), (1,)), ((), ())), preferred_element_type=jnp.float32
    )


def pack_gram(total, vectors):
    upper = total[:vectors] + total[vectors:]
    full = upper[:, :vectors] + upper[:, vectors:]
    return jnp.concatenate([full[8 * i : 8 * i + 8] for i in range(vectors // 8)], axis=1)


def iota(shape, axis):
    return lax.broadcasted_iota(jnp.int32, shape, axis)


def column(row):
    n = row.shape[1]
    return jnp.sum(jnp.where(iota((n, n), 0) == iota((n, n), 1), row, 0), axis=1, keepdims=True)


def step_kernel(
    n_row,
    n_col,
    panel,
    order,
    slot_list,
    blocks,
    source,
    product,
    inverse,
    source_in,
    held,
    held_blocks,
    c_out,
    c_in,
    c_back,
    r_out,
    r_in,
    terms,
    runs,
    ask,
    mine,
    lists_v,
    asked_v,
    sort_v,
    stack,
    gram,
    gram_row,
    gram_col,
    gram_all,
    mine_s,
    lists,
    asked,
    sort_s,
    own,
    l_send,
    l_recv,
    a_send,
    a_recv,
    c_send,
    c_recv,
    cb_send,
    cb_recv,
    r_send,
    r_recv,
    rb_send,
    rb_recv,
    gr_send,
    gr_recv,
    gc_send,
    gc_recv,
    g_send,
    g_recv,
):
    slots, size = held_blocks.shape[0], held_blocks.shape[1]
    vectors = held.shape[1]
    share = slots // n_col
    per = n_col // GROUPS
    piece = per * share
    my_row, my_col = lax.axis_index("row"), lax.axis_index("col")
    base = my_row * panel
    f32, bf16 = jnp.float32, jnp.bfloat16

    load_source = pltpu.make_async_copy(source, source_in, own.at[0])
    load_blocks = pltpu.make_async_copy(blocks, held_blocks, own.at[1])
    load_source.start()
    load_blocks.start()

    def col_peer(d):
        return partner(my_col, d, n_col)

    def row_peer(e):
        return partner(my_row, e, n_row)

    def remote(src, dst, send, recv, row, col):
        return pltpu.make_async_remote_copy(
            src_ref=src,
            dst_ref=dst,
            send_sem=send,
            recv_sem=recv,
            device_id=(row, col),
            device_id_type=MESH,
        )

    barrier = pltpu.get_barrier_semaphore()
    for d in range(1, n_col):
        pl.semaphore_signal(barrier, inc=1, device_id=(my_row, col_peer(d)), device_id_type=MESH)
    for e in range(1, n_row):
        pl.semaphore_signal(barrier, inc=1, device_id=(row_peer(e), my_col), device_id_type=MESH)

    lane = iota((1, slots), 1)

    def one_slot(i, carry):
        rows, cols = carry
        here = lane == i
        return jnp.where(here, slot_list[0, i], rows), jnp.where(here, slot_list[0, slots + i], cols)

    nothing = jnp.zeros((1, slots), jnp.int32)
    rows, cols = lax.fori_loop(0, slots, one_slot, (nothing, nothing), unroll=8)

    shift = panel.bit_length() - 1
    owner = lax.shift_right_logical(rows, shift)
    owner_c = column(owner)
    before = iota((slots, slots), 0) < iota((slots, slots), 1)
    rank = jnp.sum(jnp.where((owner_c == owner) & before, 1, 0), axis=0, keepdims=True)
    rank_c = column(rank)
    place_c = owner_c * share + rank_c
    ids = iota((slots, 1), 0)
    live = ids < slot_list[0, 2 * slots]
    row_c = jnp.where(live, column(rows & (panel - 1)) + 1, 0)
    col_c = jnp.where(live, column(cols) + 1, 0)
    lanes = iota((slots, LANES), 1)
    here = place_c == lanes
    mine[0] = jnp.sum(jnp.where(here, ids, 0), axis=0, keepdims=True)
    mine[1] = jnp.sum(jnp.where(here, col_c, 0), axis=0, keepdims=True)
    mine_place = rank_c == lanes - my_col * share
    for o in range(n_col):
        ask[o] = jnp.sum(
            jnp.where(mine_place & (owner_c == o), row_c, 0), axis=0, keepdims=True
        )
    take_mine = pltpu.make_async_copy(mine, mine_s, own.at[2])
    take_mine.start()
    lists_v[my_col] = ask[my_col]
    asked_v[my_row] = mine[1]

    load_source.wait()
    for b in range(panel):
        held[b] = source_in[:, b * size : (b + 1) * size].astype(bf16)

    pl.semaphore_wait(barrier, n_col + n_row - 2)

    def row_ask(e):
        p = row_peer(e)
        return remote(
            mine.at[1], asked_v.at[my_row], a_send.at[e], a_recv.at[e], p, my_col
        )

    def col_ask(d):
        q = col_peer(d)
        return remote(
            ask.at[q], lists_v.at[my_col], l_send.at[d], l_recv.at[d], my_row, q
        )

    def first_peer(g):
        return partner(lax.div(my_col, per), g, GROUPS) * per

    def take_lists(g):
        at = pl.ds(first_peer(g), per)
        return pltpu.make_async_copy(lists_v.at[at], lists.at[at], own.at[5 + g])

    take_asked = pltpu.make_async_copy(asked_v, asked, own.at[4])
    for e in range(1, n_row):
        row_ask(e).start()
    for d in reversed(range(1, n_col)):
        col_ask(d).start()
    take_mine.wait()
    for e in range(1, n_row):
        row_ask(e).wait()
    take_asked.start()
    take_asked.wait()

    def first_slot(g):
        return first_peer(g) * share

    def row_copy(g, e):
        at = pl.ds(first_slot(g), piece)
        p = row_peer(e)
        return remote(
            r_out.at[e, at], r_in.at[e, at], r_send.at[e, g], r_recv.at[e, g], p, my_col
        )

    def row_back(g, e):
        at = pl.ds(slots + my_row * slots + first_slot(g), piece)
        p = row_peer(e)
        return remote(
            terms.at[at], terms.at[at], rb_send.at[e, g], rb_recv.at[e, g], p, my_col
        )

    def col_copy(d):
        return remote(
            c_out.at[d], c_in.at[d], c_send.at[d], c_recv.at[d], my_row, col_peer(d)
        )

    def col_back(d):
        at = pl.ds(my_col * share, share)
        return remote(
            c_back.at[d], terms.at[at], cb_send.at[d], cb_recv.at[d], my_row, col_peer(d)
        )

    def gather(first):
        def block(at):
            if first:
                return held[at]
            return total_of(at).astype(bf16)

        for g in ORDER:
            for e in range(1, n_row):
                p, start = row_peer(e), first_slot(g)

                def one_r(n, carry):
                    at = asked[p, 0, start + n] - 1 - base
                    r_out[e, start + n] = block(jnp.clip(at, 0, panel - 1))
                    return carry

                lax.fori_loop(0, piece, one_r, 0, unroll=8)
                row_copy(g, e).start()
        for g in ORDER:
            if first:
                for d in reversed(range(max(g * per, 1), (g + 1) * per)):
                    col_ask(d).wait()
                take_lists(g).start()
                take_lists(g).wait()

            def one_c(i, carry):
                d = (g + 1) * per - 1 - i
                q = col_peer(d)
                for a in range(share):
                    at = jnp.maximum(lists[q, 0, q * share + a] - 1, 0)
                    c_out[d, a] = block(at)
                col_copy(d).start()
                return carry

            lax.fori_loop(0, per if g else per - 1, one_c, 0)
        for a in range(share):
            at = jnp.maximum(lists[my_col, 0, my_col * share + a] - 1, 0)
            c_in[0, a] = block(at)

    def multiply(between=None):
        for g in ORDER:
            if between is not None and g == ORDER[1]:
                between()
            for e in range(1, n_row):
                row_copy(g, e).wait()

            def one_peer(i, carry, own_terms=False):
                d = (g + 1) * per - 1 - i
                q = my_col if own_terms else col_peer(d)
                if not own_terms:
                    col_copy(d).wait()
                for a in range(share):
                    t = q * share + a
                    block = held_blocks[mine_s[0, 0, t]]
                    col = mine_s[1, 0, t] - 1
                    x_col = held[jnp.clip(col - base, 0, panel - 1)]
                    for e in range(1, n_row):
                        first_col = row_peer(e) * panel
                        there = (col >= first_col) & (col < first_col + panel)
                        x_col = jnp.where(there, r_in[e, t], x_col)
                    row_product = lax.dot_general(
                        x_col, block, (((1,), (1,)), ((), ())), preferred_element_type=f32
                    )
                    col_product = jnp.dot(c_in[d, a], block, preferred_element_type=f32)
                    if own_terms:
                        terms[t] = row_product.astype(bf16)
                    else:
                        c_back[d, a] = row_product.astype(bf16)
                    terms[slots + my_row * slots + t] = col_product.astype(bf16)
                if not own_terms:
                    col_back(d).start()
                return carry

            lax.fori_loop(0, per if g else per - 1, one_peer, 0)
            if g == 0:
                one_peer(per - 1, 0, own_terms=True)
            for e in range(1, n_row):
                row_back(g, e).start()

    def wait_terms():
        for g in ORDER:
            for e in range(1, n_row):
                row_back(g, e).wait()

        def one(i, carry):
            col_back(n_col - 1 - i).wait()
            return carry

        lax.fori_loop(0, n_col - 1, one, 0)

    term_count = slots * (n_row + 1)
    sort_rows = -(-term_count // LANES)

    def sort_terms():
        key_parts = []
        found = jnp.sum(lists_v[...], axis=0)
        key_parts.append(jnp.where(found > 0, found - 1, NO_KEY)[:, :slots])
        for p in range(n_row):
            at = asked_v[p] - 1 - base
            key_parts.append(jnp.where((at >= 0) & (at < panel), at, NO_KEY)[:, :slots])
        tail = sort_rows * LANES - term_count
        if tail:
            key_parts.append(jnp.full((1, tail), NO_KEY, jnp.int32))
        key = jnp.concatenate(key_parts, axis=1)
        total = sort_rows * LANES
        key_c = column(key)
        ids_c, ids_r = iota((total, total), 0), iota((total, total), 1)
        twin = (key_c == key) & (ids_c < ids_r)
        rank = jnp.sum(jnp.where(twin | (key_c < key), 1, 0), axis=0, keepdims=True)
        again = jnp.sum(jnp.where(twin, 1, 0), axis=0, keepdims=True)
        here = column(rank) == ids_r
        by_place = jnp.sum(jnp.where(here, ids_c, 0), axis=0, keepdims=True)
        goes_on = jnp.sum(jnp.where(here, column(again), 0), axis=0, keepdims=True)
        for i in range(sort_rows):
            sort_v[i] = by_place[:, i * LANES : (i + 1) * LANES]
            sort_v[sort_rows + i] = goes_on[:, i * LANES : (i + 1) * LANES]
        target = iota((total, LANES), 1)
        up_to = jnp.sum(jnp.where(key_c <= target, 1, 0), axis=0, keepdims=True)
        at_it = jnp.sum(jnp.where(key_c == target, 1, 0), axis=0, keepdims=True)
        sort_v[2 * sort_rows] = jnp.where(at_it > 0, up_to, 0)

    def add_terms():
        run = jnp.zeros((vectors, size), f32)
        for i in range(sort_rows):
            count = min(LANES, term_count - i * LANES)

            def one(n, run):
                term = terms[sort_s[i, 0, n]].astype(f32)
                run = jnp.where(sort_s[sort_rows + i, 0, n] > 0, run + term, term)
                runs[i * LANES + n] = run
                return run

            run = lax.fori_loop(0, count, one, run, unroll=8)

    def total_of(b):
        last = sort_s[2 * sort_rows, 0, b]
        return jnp.where(last > 0, runs[jnp.maximum(last - 1, 0)], 0.0)

    def gram_rows(e):
        p = row_peer(e)
        return remote(
            gram.at[0], gram_row.at[my_row], gr_send.at[e], gr_recv.at[e], p, my_col
        )

    def gram_cols(d):
        q = col_peer(d)
        return remote(
            gram.at[1], gram_col.at[my_col], gc_send.at[d], gc_recv.at[d], my_row, q
        )

    me = my_row * n_col + my_col

    def gram_copy(e, d):
        at = e * n_col + d
        p, q = row_peer(e), col_peer(d)
        return remote(gram.at[2], gram_all.at[me], g_send.at[at], g_recv.at[at], p, q)

    def send_first(total):
        packed = pack_gram(total, vectors)
        gram[0] = packed
        for e in range(1, n_row):
            gram_rows(e).start()
        gram_row[my_row] = packed

    def pass_first():
        for e in range(1, n_row):
            gram_rows(e).wait()
        partial = jnp.sum(gram_row[...], axis=0)
        gram[1] = partial
        for d in reversed(range(1, n_col)):
            gram_cols(d).start()
        gram_col[my_col] = partial

    def take_first_sum():
        for d in range(1, n_col):
            gram_cols(d).wait()
        return jnp.sum(gram_col[...], axis=0) / order

    others = [(e, d) for e in range(n_row) for d in range(n_col) if e or d][::-1]

    def sum_second(total):
        packed = pack_gram(total, vectors)
        gram[2] = packed
        for e, d in others:
            gram_copy(e, d).start()
        gram_all[me] = packed
        for e, d in others:
            gram_copy(e, d).wait()
        return jnp.sum(gram_all[...], axis=0) / order

    no_gram = jnp.zeros((2 * vectors, 2 * vectors), f32)

    gather(True)
    sort_terms()
    copy_sort = pltpu.make_async_copy(sort_v, sort_s, own.at[4])
    copy_sort.start()
    load_blocks.wait()
    multiply()
    copy_sort.wait()
    wait_terms()
    add_terms()

    gather(False)

    def take_first(i, total):
        both = jnp.concatenate([total_of(2 * i), total_of(2 * i + 1)], axis=1)
        held[2 * i] = both[:, :size].astype(bf16)
        held[2 * i + 1] = both[:, size:].astype(bf16)
        return total + gram_term(both)

    total = lax.fori_loop(0, panel // 2, take_first, no_gram, unroll=8)
    send_first(total)
    multiply(pass_first)
    stack[...] = inverse_stack(factor_inverse(take_first_sum(), vectors))
    wait_terms()
    add_terms()
    stacked = stack[...]

    def take_second(i, total):
        both = jnp.concatenate([total_of(2 * i), total_of(2 * i + 1)], axis=1)
        both = apply_inverse(stacked, both)
        product[2 * i] = both[:, :size]
        product[2 * i + 1] = both[:, size:]
        return total + gram_term(both)

    total = lax.fori_loop(0, panel // 2, take_second, no_gram, unroll=8)
    inverse[...] = factor_inverse(sum_second(total), vectors)


def finish_kernel(chunks, source, inverse, out, done, sems):
    stacked = inverse_stack(inverse[...])
    pairs, wide = source.shape[0] // 2 // chunks, out.shape[1] // chunks

    def store(j):
        at = pl.ds(j * wide, wide)
        return pltpu.make_async_copy(done.at[:, at], out.at[:, at], sems.at[j])

    for j in range(chunks):
        for i in range(j * pairs, (j + 1) * pairs):
            done[:, i * 256 : (i + 1) * 256] = apply_inverse(stacked, pair(source, i))
        store(j).start()
    for j in range(chunks):
        store(j).wait()


def per_device(n_row, n_col, blocks, block_rows, block_cols, counts, start_vectors):
    slots, size = blocks.shape[0], blocks.shape[1]
    vectors, width = start_vectors.shape
    panel = width // size
    share = slots // n_col
    f32, bf16, i32 = jnp.float32, jnp.bfloat16, jnp.int32
    shape = jax.ShapeDtypeStruct
    dma = pltpu.SemaphoreType.DMA
    gram_shape = (8, vectors * vectors // 8)
    order = float(n_row * n_col * width)
    terms = slots * (n_row + 1)
    sort_shape = (2 * (-(-terms // LANES)) + 1, 1, LANES)
    by_owner = (n_col, share, vectors, size)
    slot_list = jnp.concatenate([block_rows, block_cols, counts], axis=1)
    product, inverse = pl.pallas_call(
        functools.partial(step_kernel, n_row, n_col, panel, order),
        out_shape=(shape((panel, vectors, size), f32), shape((vectors, vectors), f32)),
        in_specs=[SMEM, ANY, ANY],
        out_specs=(VMEM, VMEM),
        scratch_shapes=[
            pltpu.VMEM((vectors, width), f32),
            pltpu.VMEM((panel, vectors, size), bf16),
            pltpu.VMEM(blocks.shape, bf16),
            pltpu.VMEM(by_owner, bf16),
            pltpu.VMEM(by_owner, bf16),
            pltpu.VMEM(by_owner, bf16),
            pltpu.VMEM((n_row, slots, vectors, size), bf16),
            pltpu.VMEM((n_row, slots, vectors, size), bf16),
            pltpu.VMEM((terms, vectors, size), bf16),
            pltpu.VMEM((terms, vectors, size), f32),
            pltpu.VMEM((n_col, 1, LANES), i32),
            pltpu.VMEM((2, 1, LANES), i32),
            pltpu.VMEM((n_col, 1, LANES), i32),
            pltpu.VMEM((n_row, 1, LANES), i32),
            pltpu.VMEM(sort_shape, i32),
            pltpu.VMEM((vectors, 4 * vectors), bf16),
            pltpu.VMEM((3,) + gram_shape, f32),
            pltpu.VMEM((n_row,) + gram_shape, f32),
            pltpu.VMEM((n_col,) + gram_shape, f32),
            pltpu.VMEM((n_row * n_col,) + gram_shape, f32),
            pltpu.SMEM((2, 1, LANES), i32),
            pltpu.SMEM((n_col, 1, LANES), i32),
            pltpu.SMEM((n_row, 1, LANES), i32),
            pltpu.SMEM(sort_shape, i32),
            dma((5 + GROUPS,)),
            dma((n_col,)),
            dma((n_col,)),
            dma((n_row,)),
            dma((n_row,)),
            dma((n_col,)),
            dma((n_col,)),
            dma((n_col,)),
            dma((n_col,)),
            dma((n_row, GROUPS)),
            dma((n_row, GROUPS)),
            dma((n_row, GROUPS)),
            dma((n_row, GROUPS)),
            dma((n_row,)),
            dma((n_row,)),
            dma((n_col,)),
            dma((n_col,)),
            dma((n_row * n_col,)),
            dma((n_row * n_col,)),
        ],
        compiler_params=pltpu.CompilerParams(
            collective_id=1, has_side_effects=True, vmem_limit_bytes=KERNEL_BYTES
        ),
    )(slot_list, blocks, start_vectors)
    chunks = min(8, panel // 2)
    return pl.pallas_call(
        functools.partial(finish_kernel, chunks),
        out_shape=shape((vectors, width), f32),
        in_specs=[VMEM, VMEM],
        out_specs=ANY,
        scratch_shapes=[pltpu.VMEM((vectors, width), f32), dma((chunks,))],
        compiler_params=pltpu.CompilerParams(vmem_limit_bytes=KERNEL_BYTES),
    )(product, inverse)


def solution(mesh):
    placed = (
        P("row", "col", None),
        P("row", "col"),
        P("row", "col"),
        P("row", "col"),
        P(None, ("row", "col")),
    )
    return jax.shard_map(
        functools.partial(per_device, mesh.shape["row"], mesh.shape["col"]),
        mesh=mesh,
        in_specs=placed,
        out_specs=P(None, ("row", "col")),
        check_vma=False,
    )
```

```python
import functools

import jax
import jax.numpy as jnp
from jax import lax
from jax.experimental import pallas as pl
from jax.experimental.pallas import tpu as pltpu
from jax.sharding import PartitionSpec as P

ITERS = 2
GROUPS = 4
ORDER = (3, 1, 2, 0)
LANES = 128
MESH = pl.DeviceIdType.MESH
ANY = pl.BlockSpec(memory_space=pl.ANY)
VMEM = pl.BlockSpec(memory_space=pltpu.VMEM)
KERNEL_BYTES = 50 << 20
NO_KEY = 1 << 20


def partner(me, d, size):
    other, w = 0, 1
    while w < size:
        step = d // w if isinstance(d, int) else lax.div(d, w)
        other = other + w * lax.rem(lax.div(me, w) + step, 2)
        w *= 2
    return other


def split(value):
    high = value.astype(jnp.bfloat16)
    return high, (value - high.astype(jnp.float32)).astype(jnp.bfloat16)


def inverse_stack(inverse):
    high, low = split(inverse)
    return jnp.concatenate([high, low, high, low], axis=1)


def pair(blocks, i):
    return jnp.concatenate([blocks[2 * i], blocks[2 * i + 1]], axis=1)


def apply_inverse(stacked, product):
    high, low = split(product)
    parts = jnp.concatenate([high, high, low, low], axis=0)
    return jnp.dot(stacked, parts, preferred_element_type=jnp.float32)


def factor_inverse(packed, size):
    full = jnp.concatenate([packed[:, size * i : size * (i + 1)] for i in range(size // 8)], axis=0)
    rows = lax.broadcasted_iota(jnp.int32, (size, size), 0)
    lanes = lax.broadcasted_iota(jnp.int32, (size, size), 1)
    work = jnp.concatenate([full, (rows == lanes).astype(jnp.float32)], axis=1)
    row_ids = lax.broadcasted_iota(jnp.int32, work.shape, 0)
    for j in range(0, size, 8):
        columns = [jnp.broadcast_to(work[:, j + k : j + k + 1], work.shape) for k in range(8)]
        pivot_rows = [work[j + k : j + k + 1, :] for k in range(8)]
        for k in range(8):
            at = j + k
            scale = 1.0 / columns[k][at : at + 1, :]
            pivot_row = pivot_rows[k] * scale
            for m in range(k + 1, 8):
                factor = columns[m][at : at + 1, :] * scale
                pivot_rows[m] = pivot_rows[m] - columns[k][j + m : j + m + 1, :] * pivot_row
                columns[m] = columns[m] - columns[k] * factor
            work = work - jnp.where(row_ids > at, columns[k], 0.0) * pivot_row
    pivots = jnp.sum(jnp.where(rows == lanes, work[:, :size], 0.0), axis=1, keepdims=True)
    return work[:, size:] * (1.0 / jnp.sqrt(pivots))


def gram_term(value):
    high, low = split(value)
    parts = jnp.concatenate([high, low], axis=0)
    return lax.dot_general(
        parts, parts, (((1,), (1,)), ((), ())), preferred_element_type=jnp.float32
    )


def pack_gram(total, vectors):
    upper = total[:vectors] + total[vectors:]
    full = upper[:, :vectors] + upper[:, vectors:]
    return jnp.concatenate([full[8 * i : 8 * i + 8] for i in range(vectors // 8)], axis=1)


def iota(shape, axis):
    return lax.broadcasted_iota(jnp.int32, shape, axis)


def column(row):
    n = row.shape[1]
    return jnp.sum(jnp.where(iota((n, n), 0) == iota((n, n), 1), row, 0), axis=1, keepdims=True)


def step_kernel(
    n_row,
    n_col,
    panel,
    order,
    slot_list,
    blocks,
    source,
    product,
    inverse,
    source_in,
    held,
    held_blocks,
    c_out,
    c_in,
    c_back,
    r_out,
    r_in,
    terms,
    runs,
    ask,
    mine,
    lists_v,
    asked_v,
    sort_v,
    stack,
    gram,
    gram_row,
    gram_col,
    gram_all,
    mine_s,
    lists,
    asked,
    sort_s,
    own,
    l_send,
    l_recv,
    a_send,
    a_recv,
    c_send,
    c_recv,
    cb_send,
    cb_recv,
    r_send,
    r_recv,
    rb_send,
    rb_recv,
    gr_send,
    gr_recv,
    gc_send,
    gc_recv,
    g_send,
    g_recv,
):
    slots, size = held_blocks.shape[0], held_blocks.shape[1]
    vectors = held.shape[1]
    share = slots // n_col
    per = n_col // GROUPS
    piece = per * share
    my_row, my_col = lax.axis_index("row"), lax.axis_index("col")
    base = my_row * panel
    f32, bf16 = jnp.float32, jnp.bfloat16

    load_source = pltpu.make_async_copy(source, source_in, own.at[0])
    load_blocks = pltpu.make_async_copy(blocks, held_blocks, own.at[1])

    def col_peer(d):
        return partner(my_col, d, n_col)

    def row_peer(e):
        return partner(my_row, e, n_row)

    def remote(src, dst, send, recv, row, col):
        return pltpu.make_async_remote_copy(
            src_ref=src,
            dst_ref=dst,
            send_sem=send,
            recv_sem=recv,
            device_id=(row, col),
            device_id_type=MESH,
        )

    barrier = pltpu.get_barrier_semaphore()
    for d in range(1, n_col):
        pl.semaphore_signal(barrier, inc=1, device_id=(my_row, col_peer(d)), device_id_type=MESH)
    for e in range(1, n_row):
        pl.semaphore_signal(barrier, inc=1, device_id=(row_peer(e), my_col), device_id_type=MESH)

    load_source.start()
    load_blocks.start()
    rows, cols = slot_list[:, :slots], slot_list[:, slots : 2 * slots]

    shift = panel.bit_length() - 1
    owner = lax.shift_right_logical(rows, shift)
    owner_c = column(owner)
    before = iota((slots, slots), 0) < iota((slots, slots), 1)
    rank = jnp.sum(jnp.where((owner_c == owner) & before, 1, 0), axis=0, keepdims=True)
    rank_c = column(rank)
    place_c = owner_c * share + rank_c
    ids = iota((slots, 1), 0)
    live = ids < slot_list[:, 2 * slots : 2 * slots + 1]
    row_c = jnp.where(live, column(rows & (panel - 1)) + 1, 0)
    col_c = jnp.where(live, column(cols) + 1, 0)
    lanes = iota((slots, LANES), 1)
    here = place_c == lanes
    mine[0] = jnp.sum(jnp.where(here, ids, 0), axis=0, keepdims=True)
    mine[1] = jnp.sum(jnp.where(here, col_c, 0), axis=0, keepdims=True)
    mine_place = rank_c == lanes - my_col * share
    for o in range(n_col):
        ask[o] = jnp.sum(
            jnp.where(mine_place & (owner_c == o), row_c, 0), axis=0, keepdims=True
        )
    take_mine = pltpu.make_async_copy(mine, mine_s, own.at[2])
    take_mine.start()
    lists_v[my_col] = ask[my_col]
    asked_v[my_row] = mine[1]

    load_source.wait()
    for b in range(panel):
        held[b] = source_in[:, b * size : (b + 1) * size].astype(bf16)

    pl.semaphore_wait(barrier, n_col + n_row - 2)

    def row_ask(e):
        p = row_peer(e)
        return remote(
            mine.at[1], asked_v.at[my_row], a_send.at[e], a_recv.at[e], p, my_col
        )

    def col_ask(d):
        q = col_peer(d)
        return remote(
            ask.at[q], lists_v.at[my_col], l_send.at[d], l_recv.at[d], my_row, q
        )

    def first_peer(g):
        return partner(lax.div(my_col, per), g, GROUPS) * per

    def take_lists(g):
        at = pl.ds(first_peer(g), per)
        return pltpu.make_async_copy(lists_v.at[at], lists.at[at], own.at[5 + g])

    take_asked = pltpu.make_async_copy(asked_v, asked, own.at[4])
    for e in range(1, n_row):
        row_ask(e).start()
    for d in reversed(range(1, n_col)):
        col_ask(d).start()
    take_mine.wait()
    for e in range(1, n_row):
        row_ask(e).wait()
    take_asked.start()
    take_asked.wait()

    def first_slot(g):
        return first_peer(g) * share

    def row_copy(g, e):
        at = pl.ds(first_slot(g), piece)
        p = row_peer(e)
        return remote(
            r_out.at[e, at], r_in.at[e, at], r_send.at[e, g], r_recv.at[e, g], p, my_col
        )

    def row_back(g, e):
        at = pl.ds(slots + my_row * slots + first_slot(g), piece)
        p = row_peer(e)
        return remote(
            terms.at[at], terms.at[at], rb_send.at[e, g], rb_recv.at[e, g], p, my_col
        )

    def col_copy(d):
        return remote(
            c_out.at[d], c_in.at[d], c_send.at[d], c_recv.at[d], my_row, col_peer(d)
        )

    def col_back(d):
        at = pl.ds(my_col * share, share)
        return remote(
            c_back.at[d], terms.at[at], cb_send.at[d], cb_recv.at[d], my_row, col_peer(d)
        )

    def gather(first):
        def block(at):
            if first:
                return held[at]
            return total_of(at).astype(bf16)

        def gather_rows(g):
            for e in range(1, n_row):
                p, start = row_peer(e), first_slot(g)

                def one_r(n, carry):
                    at = asked[p, 0, start + n] - 1 - base
                    r_out[e, start + n] = block(jnp.clip(at, 0, panel - 1))
                    return carry

                lax.fori_loop(0, piece, one_r, 0, unroll=8)
                row_copy(g, e).start()

        def gather_cols(g):
            if first:
                for d in reversed(range(max(g * per, 1), (g + 1) * per)):
                    col_ask(d).wait()
                take_lists(g).start()
                take_lists(g).wait()

            def one_c(i, carry):
                d = (g + 1) * per - 1 - i
                q = col_peer(d)
                for a in range(share):
                    at = jnp.maximum(lists[q, 0, q * share + a] - 1, 0)
                    c_out[d, a] = block(at)
                col_copy(d).start()
                return carry

            lax.fori_loop(0, per if g else per - 1, one_c, 0)

        for g in ORDER:
            gather_rows(g)
            gather_cols(g)
        for a in range(share):
            at = jnp.maximum(lists[my_col, 0, my_col * share + a] - 1, 0)
            c_in[0, a] = block(at)

    def multiply(between=None):
        for g in ORDER:
            if between is not None and g == ORDER[1]:
                between()
            for e in range(1, n_row):
                row_copy(g, e).wait()

            def one_peer(i, carry, own_terms=False):
                d = (g + 1) * per - 1 - i
                q = my_col if own_terms else col_peer(d)
                if not own_terms:
                    col_copy(d).wait()
                for a in range(share):
                    t = q * share + a
                    block = held_blocks[mine_s[0, 0, t]]
                    col = mine_s[1, 0, t] - 1
                    x_col = held[jnp.clip(col - base, 0, panel - 1)]
                    for e in range(1, n_row):
                        first_col = row_peer(e) * panel
                        there = (col >= first_col) & (col < first_col + panel)
                        x_col = jnp.where(there, r_in[e, t], x_col)
                    row_product = lax.dot_general(
                        x_col, block, (((1,), (1,)), ((), ())), preferred_element_type=f32
                    )
                    col_product = jnp.dot(c_in[d, a], block, preferred_element_type=f32)
                    if own_terms:
                        terms[t] = row_product.astype(bf16)
                    else:
                        c_back[d, a] = row_product.astype(bf16)
                    terms[slots + my_row * slots + t] = col_product.astype(bf16)
                if not own_terms:
                    col_back(d).start()
                return carry

            lax.fori_loop(0, per if g else per - 1, one_peer, 0)
            if g == 0:
                one_peer(per - 1, 0, own_terms=True)
            for e in range(1, n_row):
                row_back(g, e).start()

    def wait_terms():
        for g in ORDER:
            for e in range(1, n_row):
                row_back(g, e).wait()

        def one(i, carry):
            col_back(n_col - 1 - i).wait()
            return carry

        lax.fori_loop(0, n_col - 1, one, 0)

    term_count = slots * (n_row + 1)
    sort_rows = -(-term_count // LANES)

    def sort_terms():
        key_parts = []
        found = jnp.sum(lists_v[...], axis=0)
        key_parts.append(jnp.where(found > 0, found - 1, NO_KEY)[:, :slots])
        for p in range(n_row):
            at = asked_v[p] - 1 - base
            key_parts.append(jnp.where((at >= 0) & (at < panel), at, NO_KEY)[:, :slots])
        tail = sort_rows * LANES - term_count
        if tail:
            key_parts.append(jnp.full((1, tail), NO_KEY, jnp.int32))
        key = jnp.concatenate(key_parts, axis=1)
        total = sort_rows * LANES
        key_c = column(key)
        ids_c, ids_r = iota((total, total), 0), iota((total, total), 1)
        twin = (key_c == key) & (ids_c < ids_r)
        rank = jnp.sum(jnp.where(twin | (key_c < key), 1, 0), axis=0, keepdims=True)
        again = jnp.sum(jnp.where(twin, 1, 0), axis=0, keepdims=True)
        here = column(rank) == ids_r
        by_place = jnp.sum(jnp.where(here, ids_c, 0), axis=0, keepdims=True)
        goes_on = jnp.sum(jnp.where(here, column(again), 0), axis=0, keepdims=True)
        for i in range(sort_rows):
            sort_v[i] = by_place[:, i * LANES : (i + 1) * LANES]
            sort_v[sort_rows + i] = goes_on[:, i * LANES : (i + 1) * LANES]
        target = iota((total, LANES), 1)
        up_to = jnp.sum(jnp.where(key_c <= target, 1, 0), axis=0, keepdims=True)
        at_it = jnp.sum(jnp.where(key_c == target, 1, 0), axis=0, keepdims=True)
        sort_v[2 * sort_rows] = jnp.where(at_it > 0, up_to, 0)

    def add_terms():
        run = jnp.zeros((vectors, size), f32)
        for i in range(sort_rows):
            count = min(LANES, term_count - i * LANES)

            def one(n, run):
                term = terms[sort_s[i, 0, n]].astype(f32)
                run = jnp.where(sort_s[sort_rows + i, 0, n] > 0, run + term, term)
                runs[i * LANES + n] = run
                return run

            run = lax.fori_loop(0, count, one, run, unroll=8)

    def total_of(b):
        last = sort_s[2 * sort_rows, 0, b]
        return jnp.where(last > 0, runs[jnp.maximum(last - 1, 0)], 0.0)

    def gram_rows(e):
        p = row_peer(e)
        return remote(
            gram.at[0], gram_row.at[my_row], gr_send.at[e], gr_recv.at[e], p, my_col
        )

    def gram_cols(d):
        q = col_peer(d)
        return remote(
            gram.at[1], gram_col.at[my_col], gc_send.at[d], gc_recv.at[d], my_row, q
        )

    me = my_row * n_col + my_col

    def gram_copy(e, d):
        at = e * n_col + d
        p, q = row_peer(e), col_peer(d)
        return remote(gram.at[2], gram_all.at[me], g_send.at[at], g_recv.at[at], p, q)

    def send_first(total):
        packed = pack_gram(total, vectors)
        gram[0] = packed
        for e in range(1, n_row):
            gram_rows(e).start()
        gram_row[my_row] = packed

    def pass_first():
        for e in range(1, n_row):
            gram_rows(e).wait()
        partial = jnp.sum(gram_row[...], axis=0)
        gram[1] = partial
        for d in reversed(range(1, n_col)):
            gram_cols(d).start()
        gram_col[my_col] = partial

    def take_first_sum():
        for d in range(1, n_col):
            gram_cols(d).wait()
        return jnp.sum(gram_col[...], axis=0) / order

    others = [(e, d) for e in range(n_row) for d in range(n_col) if e or d][::-1]

    def sum_second(total):
        packed = pack_gram(total, vectors)
        gram[2] = packed
        for e, d in others:
            gram_copy(e, d).start()
        gram_all[me] = packed
        for e, d in others:
            gram_copy(e, d).wait()
        return jnp.sum(gram_all[...], axis=0) / order

    no_gram = jnp.zeros((2 * vectors, 2 * vectors), f32)

    gather(True)
    sort_terms()
    copy_sort = pltpu.make_async_copy(sort_v, sort_s, own.at[4])
    copy_sort.start()
    load_blocks.wait()
    multiply()
    copy_sort.wait()
    wait_terms()
    add_terms()

    gather(False)

    def take_first(i, total):
        both = jnp.concatenate([total_of(2 * i), total_of(2 * i + 1)], axis=1)
        held[2 * i] = both[:, :size].astype(bf16)
        held[2 * i + 1] = both[:, size:].astype(bf16)
        return total + gram_term(both)

    total = lax.fori_loop(0, panel // 2, take_first, no_gram, unroll=8)
    send_first(total)
    multiply(pass_first)
    stack[...] = inverse_stack(factor_inverse(take_first_sum(), vectors))
    wait_terms()
    add_terms()
    stacked = stack[...]

    def take_second(i, total):
        both = jnp.concatenate([total_of(2 * i), total_of(2 * i + 1)], axis=1)
        both = apply_inverse(stacked, both)
        product[2 * i] = both[:, :size]
        product[2 * i + 1] = both[:, size:]
        return total + gram_term(both)

    total = lax.fori_loop(0, panel // 2, take_second, no_gram, unroll=8)
    inverse[...] = factor_inverse(sum_second(total), vectors)


def finish_kernel(chunks, source, inverse, out, done, sems):
    stacked = inverse_stack(inverse[...])
    pairs, wide = source.shape[0] // 2 // chunks, out.shape[1] // chunks

    def store(j):
        at = pl.ds(j * wide, wide)
        return pltpu.make_async_copy(done.at[:, at], out.at[:, at], sems.at[j])

    for j in range(chunks):
        for i in range(j * pairs, (j + 1) * pairs):
            done[:, i * 256 : (i + 1) * 256] = apply_inverse(stacked, pair(source, i))
        store(j).start()
    for j in range(chunks):
        store(j).wait()


def per_device(n_row, n_col, blocks, block_rows, block_cols, counts, start_vectors):
    slots, size = blocks.shape[0], blocks.shape[1]
    vectors, width = start_vectors.shape
    panel = width // size
    share = slots // n_col
    f32, bf16, i32 = jnp.float32, jnp.bfloat16, jnp.int32
    shape = jax.ShapeDtypeStruct
    dma = pltpu.SemaphoreType.DMA
    gram_shape = (8, vectors * vectors // 8)
    order = float(n_row * n_col * width)
    terms = slots * (n_row + 1)
    sort_shape = (2 * (-(-terms // LANES)) + 1, 1, LANES)
    by_owner = (n_col, share, vectors, size)
    slot_list = jnp.concatenate([block_rows, block_cols, counts], axis=1)
    product, inverse = pl.pallas_call(
        functools.partial(step_kernel, n_row, n_col, panel, order),
        out_shape=(shape((panel, vectors, size), f32), shape((vectors, vectors), f32)),
        in_specs=[VMEM, ANY, ANY],
        out_specs=(VMEM, VMEM),
        scratch_shapes=[
            pltpu.VMEM((vectors, width), f32),
            pltpu.VMEM((panel, vectors, size), bf16),
            pltpu.VMEM(blocks.shape, bf16),
            pltpu.VMEM(by_owner, bf16),
            pltpu.VMEM(by_owner, bf16),
            pltpu.VMEM(by_owner, bf16),
            pltpu.VMEM((n_row, slots, vectors, size), bf16),
            pltpu.VMEM((n_row, slots, vectors, size), bf16),
            pltpu.VMEM((terms, vectors, size), bf16),
            pltpu.VMEM((terms, vectors, size), f32),
            pltpu.VMEM((n_col, 1, LANES), i32),
            pltpu.VMEM((2, 1, LANES), i32),
            pltpu.VMEM((n_col, 1, LANES), i32),
            pltpu.VMEM((n_row, 1, LANES), i32),
            pltpu.VMEM(sort_shape, i32),
            pltpu.VMEM((vectors, 4 * vectors), bf16),
            pltpu.VMEM((3,) + gram_shape, f32),
            pltpu.VMEM((n_row,) + gram_shape, f32),
            pltpu.VMEM((n_col,) + gram_shape, f32),
            pltpu.VMEM((n_row * n_col,) + gram_shape, f32),
            pltpu.SMEM((2, 1, LANES), i32),
            pltpu.SMEM((n_col, 1, LANES), i32),
            pltpu.SMEM((n_row, 1, LANES), i32),
            pltpu.SMEM(sort_shape, i32),
            dma((5 + GROUPS,)),
            dma((n_col,)),
            dma((n_col,)),
            dma((n_row,)),
            dma((n_row,)),
            dma((n_col,)),
            dma((n_col,)),
            dma((n_col,)),
            dma((n_col,)),
            dma((n_row, GROUPS)),
            dma((n_row, GROUPS)),
            dma((n_row, GROUPS)),
            dma((n_row, GROUPS)),
            dma((n_row,)),
            dma((n_row,)),
            dma((n_col,)),
            dma((n_col,)),
            dma((n_row * n_col,)),
            dma((n_row * n_col,)),
        ],
        compiler_params=pltpu.CompilerParams(
            collective_id=1, has_side_effects=True, vmem_limit_bytes=KERNEL_BYTES
        ),
    )(slot_list, blocks, start_vectors)
    chunks = min(8, panel // 2)
    return pl.pallas_call(
        functools.partial(finish_kernel, chunks),
        out_shape=shape((vectors, width), f32),
        in_specs=[VMEM, VMEM],
        out_specs=ANY,
        scratch_shapes=[pltpu.VMEM((vectors, width), f32), dma((chunks,))],
        compiler_params=pltpu.CompilerParams(vmem_limit_bytes=KERNEL_BYTES),
    )(product, inverse)


def solution(mesh):
    placed = (
        P("row", "col", None),
        P("row", "col"),
        P("row", "col"),
        P("row", "col"),
        P(None, ("row", "col")),
    )
    return jax.shard_map(
        functools.partial(per_device, mesh.shape["row"], mesh.shape["col"]),
        mesh=mesh,
        in_specs=placed,
        out_specs=P(None, ("row", "col")),
        check_vma=False,
    )
```

```python
import functools

import jax
import jax.numpy as jnp
from jax import lax
from jax.experimental import pallas as pl
from jax.experimental.pallas import tpu as pltpu
from jax.sharding import PartitionSpec as P

ITERS = 2
GROUPS = 4
ORDER = (3, 1, 2, 0)
LANES = 128
MESH = pl.DeviceIdType.MESH
ANY = pl.BlockSpec(memory_space=pl.ANY)
VMEM = pl.BlockSpec(memory_space=pltpu.VMEM)
KERNEL_BYTES = 50 << 20
NO_KEY = 1 << 20


def partner(me, d, size):
    other, w = 0, 1
    while w < size:
        step = d // w if isinstance(d, int) else lax.div(d, w)
        other = other + w * lax.rem(lax.div(me, w) + step, 2)
        w *= 2
    return other


def split(value):
    high = value.astype(jnp.bfloat16)
    return high, (value - high.astype(jnp.float32)).astype(jnp.bfloat16)


def inverse_stack(inverse):
    high, low = split(inverse)
    return jnp.concatenate([high, low, high, low], axis=1)


def pair(blocks, i):
    return jnp.concatenate([blocks[2 * i], blocks[2 * i + 1]], axis=1)


def apply_inverse(stacked, product):
    high, low = split(product)
    parts = jnp.concatenate([high, high, low, low], axis=0)
    return jnp.dot(stacked, parts, preferred_element_type=jnp.float32)


def factor_inverse(packed, size):
    full = jnp.concatenate([packed[:, size * i : size * (i + 1)] for i in range(size // 8)], axis=0)
    rows = lax.broadcasted_iota(jnp.int32, (size, size), 0)
    lanes = lax.broadcasted_iota(jnp.int32, (size, size), 1)
    work = jnp.concatenate([full, (rows == lanes).astype(jnp.float32)], axis=1)
    row_ids = lax.broadcasted_iota(jnp.int32, work.shape, 0)
    for j in range(0, size, 8):
        columns = [jnp.broadcast_to(work[:, j + k : j + k + 1], work.shape) for k in range(8)]
        pivot_rows = [work[j + k : j + k + 1, :] for k in range(8)]
        for k in range(8):
            at = j + k
            scale = 1.0 / columns[k][at : at + 1, :]
            pivot_row = pivot_rows[k] * scale
            for m in range(k + 1, 8):
                factor = columns[m][at : at + 1, :] * scale
                pivot_rows[m] = pivot_rows[m] - columns[k][j + m : j + m + 1, :] * pivot_row
                columns[m] = columns[m] - columns[k] * factor
            work = work - jnp.where(row_ids > at, columns[k], 0.0) * pivot_row
    pivots = jnp.sum(jnp.where(rows == lanes, work[:, :size], 0.0), axis=1, keepdims=True)
    return work[:, size:] * (1.0 / jnp.sqrt(pivots))


def gram_term(value):
    high, low = split(value)
    parts = jnp.concatenate([high, low], axis=0)
    return lax.dot_general(
        parts, parts, (((1,), (1,)), ((), ())), preferred_element_type=jnp.float32
    )


def pack_gram(total, vectors):
    upper = total[:vectors] + total[vectors:]
    full = upper[:, :vectors] + upper[:, vectors:]
    return jnp.concatenate([full[8 * i : 8 * i + 8] for i in range(vectors // 8)], axis=1)


def iota(shape, axis):
    return lax.broadcasted_iota(jnp.int32, shape, axis)


def column(row):
    n = row.shape[1]
    return jnp.sum(jnp.where(iota((n, n), 0) == iota((n, n), 1), row, 0), axis=1, keepdims=True)


def step_kernel(
    n_row,
    n_col,
    panel,
    order,
    slot_list,
    blocks,
    source,
    product,
    inverse,
    source_in,
    held,
    held_blocks,
    c_out,
    c_in,
    c_back,
    r_out,
    r_in,
    terms,
    runs,
    ask,
    mine,
    lists_v,
    asked_v,
    sort_v,
    stack,
    gram,
    gram_row,
    gram_col,
    gram_all,
    mine_s,
    lists,
    asked,
    sort_s,
    own,
    l_send,
    l_recv,
    a_send,
    a_recv,
    c_send,
    c_recv,
    cb_send,
    cb_recv,
    r_send,
    r_recv,
    rb_send,
    rb_recv,
    gr_send,
    gr_recv,
    gc_send,
    gc_recv,
    g_send,
    g_recv,
):
    slots, size = held_blocks.shape[0], held_blocks.shape[1]
    vectors = held.shape[1]
    share = slots // n_col
    per = n_col // GROUPS
    piece = per * share
    my_row, my_col = lax.axis_index("row"), lax.axis_index("col")
    base = my_row * panel
    f32, bf16 = jnp.float32, jnp.bfloat16

    load_source = pltpu.make_async_copy(source, source_in, own.at[0])
    load_blocks = pltpu.make_async_copy(blocks, held_blocks, own.at[1])

    def col_peer(d):
        return partner(my_col, d, n_col)

    def row_peer(e):
        return partner(my_row, e, n_row)

    def remote(src, dst, send, recv, row, col):
        return pltpu.make_async_remote_copy(
            src_ref=src,
            dst_ref=dst,
            send_sem=send,
            recv_sem=recv,
            device_id=(row, col),
            device_id_type=MESH,
        )

    barrier = pltpu.get_barrier_semaphore()
    for d in range(1, n_col):
        pl.semaphore_signal(barrier, inc=1, device_id=(my_row, col_peer(d)), device_id_type=MESH)
    for e in range(1, n_row):
        pl.semaphore_signal(barrier, inc=1, device_id=(row_peer(e), my_col), device_id_type=MESH)

    load_source.start()
    load_blocks.start()
    rows, cols = slot_list[:, :slots], slot_list[:, slots : 2 * slots]

    shift = panel.bit_length() - 1
    owner = lax.shift_right_logical(rows, shift)
    owner_c = column(owner)
    before = iota((slots, slots), 0) < iota((slots, slots), 1)
    rank = jnp.sum(jnp.where((owner_c == owner) & before, 1, 0), axis=0, keepdims=True)
    rank_c = column(rank)
    place_c = owner_c * share + rank_c
    ids = iota((slots, 1), 0)
    live = ids < slot_list[:, 2 * slots : 2 * slots + 1]
    row_c = jnp.where(live, column(rows & (panel - 1)) + 1, 0)
    col_c = jnp.where(live, column(cols) + 1, 0)
    lanes = iota((slots, LANES), 1)
    here = place_c == lanes
    mine[0] = jnp.sum(jnp.where(here, ids, 0), axis=0, keepdims=True)
    mine[1] = jnp.sum(jnp.where(here, col_c, 0), axis=0, keepdims=True)
    mine_place = rank_c == lanes - my_col * share
    for o in range(n_col):
        ask[o] = jnp.sum(
            jnp.where(mine_place & (owner_c == o), row_c, 0), axis=0, keepdims=True
        )
    take_mine = pltpu.make_async_copy(mine, mine_s, own.at[2])
    take_mine.start()
    lists_v[my_col] = ask[my_col]
    asked_v[my_row] = mine[1]

    load_source.wait()
    for b in range(panel):
        held[b] = source_in[:, b * size : (b + 1) * size].astype(bf16)

    pl.semaphore_wait(barrier, n_col + n_row - 2)

    def row_ask(e):
        p = row_peer(e)
        return remote(
            mine.at[1], asked_v.at[my_row], a_send.at[e], a_recv.at[e], p, my_col
        )

    def col_ask(d):
        q = col_peer(d)
        return remote(
            ask.at[q], lists_v.at[my_col], l_send.at[d], l_recv.at[d], my_row, q
        )

    def first_peer(g):
        return partner(lax.div(my_col, per), g, GROUPS) * per

    def take_lists(g):
        at = pl.ds(first_peer(g), per)
        return pltpu.make_async_copy(lists_v.at[at], lists.at[at], own.at[5 + g])

    take_asked = pltpu.make_async_copy(asked_v, asked, own.at[4])
    for e in range(1, n_row):
        row_ask(e).start()
    for d in reversed(range(1, n_col)):
        col_ask(d).start()
    take_mine.wait()
    for e in range(1, n_row):
        row_ask(e).wait()
    take_asked.start()
    take_asked.wait()

    def first_slot(g):
        return first_peer(g) * share

    def row_copy(g, e):
        at = pl.ds(first_slot(g), piece)
        p = row_peer(e)
        return remote(
            r_out.at[e, at], r_in.at[e, at], r_send.at[e, g], r_recv.at[e, g], p, my_col
        )

    def row_back(g, e):
        at = pl.ds(slots + my_row * slots + first_slot(g), piece)
        p = row_peer(e)
        return remote(
            terms.at[at], terms.at[at], rb_send.at[e, g], rb_recv.at[e, g], p, my_col
        )

    def col_copy(d):
        return remote(
            c_out.at[d], c_in.at[d], c_send.at[d], c_recv.at[d], my_row, col_peer(d)
        )

    def col_back(d):
        at = pl.ds(my_col * share, share)
        return remote(
            c_back.at[d], terms.at[at], cb_send.at[d], cb_recv.at[d], my_row, col_peer(d)
        )

    def gather(first):
        def block(at):
            if first:
                return held[at]
            return total_of(at).astype(bf16)

        def gather_rows(g):
            for e in range(1, n_row):
                p, start = row_peer(e), first_slot(g)

                def one_r(n, carry):
                    at = asked[p, 0, start + n] - 1 - base
                    r_out[e, start + n] = block(jnp.clip(at, 0, panel - 1))
                    return carry

                lax.fori_loop(0, piece, one_r, 0, unroll=8)
                row_copy(g, e).start()

        def gather_cols(g):
            if first:
                for d in reversed(range(max(g * per, 1), (g + 1) * per)):
                    col_ask(d).wait()
                take_lists(g).start()
                take_lists(g).wait()

            def one_c(i, carry):
                d = (g + 1) * per - 1 - i
                q = col_peer(d)
                for a in range(share):
                    at = jnp.maximum(lists[q, 0, q * share + a] - 1, 0)
                    c_out[d, a] = block(at)
                col_copy(d).start()
                return carry

            lax.fori_loop(0, per if g else per - 1, one_c, 0)

        for g in ORDER:
            gather_rows(g)
            gather_cols(g)
        for a in range(share):
            at = jnp.maximum(lists[my_col, 0, my_col * share + a] - 1, 0)
            c_in[0, a] = block(at)

    def multiply(between=None):
        for g in ORDER:
            if between is not None and g == ORDER[1]:
                between()
            for e in range(1, n_row):
                row_copy(g, e).wait()

            def one_peer(i, carry, own_terms=False):
                d = (g + 1) * per - 1 - i
                q = my_col if own_terms else col_peer(d)
                if not own_terms:
                    col_copy(d).wait()
                for a in range(share):
                    t = q * share + a
                    block = held_blocks[mine_s[0, 0, t]]
                    col = mine_s[1, 0, t] - 1
                    x_col = held[jnp.clip(col - base, 0, panel - 1)]
                    for e in range(1, n_row):
                        first_col = row_peer(e) * panel
                        there = (col >= first_col) & (col < first_col + panel)
                        x_col = jnp.where(there, r_in[e, t], x_col)
                    row_product = lax.dot_general(
                        x_col, block, (((1,), (1,)), ((), ())), preferred_element_type=f32
                    )
                    col_product = jnp.dot(c_in[d, a], block, preferred_element_type=f32)
                    if own_terms:
                        terms[t] = row_product.astype(bf16)
                    else:
                        c_back[d, a] = row_product.astype(bf16)
                    terms[slots + my_row * slots + t] = col_product.astype(bf16)
                if not own_terms:
                    col_back(d).start()
                return carry

            lax.fori_loop(0, per if g else per - 1, one_peer, 0)
            if g == 0:
                one_peer(per - 1, 0, own_terms=True)
            for e in range(1, n_row):
                row_back(g, e).start()

    def wait_terms():
        for g in ORDER:
            for e in range(1, n_row):
                row_back(g, e).wait()

        def one(i, carry):
            col_back(n_col - 1 - i).wait()
            return carry

        lax.fori_loop(0, n_col - 1, one, 0)

    term_count = slots * (n_row + 1)
    sort_rows = -(-term_count // LANES)

    def sort_terms():
        key_parts = []
        found = jnp.sum(lists_v[...], axis=0)
        key_parts.append(jnp.where(found > 0, found - 1, NO_KEY)[:, :slots])
        for p in range(n_row):
            at = asked_v[p] - 1 - base
            key_parts.append(jnp.where((at >= 0) & (at < panel), at, NO_KEY)[:, :slots])
        tail = sort_rows * LANES - term_count
        if tail:
            key_parts.append(jnp.full((1, tail), NO_KEY, jnp.int32))
        key = jnp.concatenate(key_parts, axis=1)
        total = sort_rows * LANES
        key_c = column(key)
        ids_c, ids_r = iota((total, total), 0), iota((total, total), 1)
        twin = (key_c == key) & (ids_c < ids_r)
        rank = jnp.sum(jnp.where(twin | (key_c < key), 1, 0), axis=0, keepdims=True)
        again = jnp.sum(jnp.where(twin, 1, 0), axis=0, keepdims=True)
        here = column(rank) == ids_r
        by_place = jnp.sum(jnp.where(here, ids_c, 0), axis=0, keepdims=True)
        goes_on = jnp.sum(jnp.where(here, column(again), 0), axis=0, keepdims=True)
        for i in range(sort_rows):
            sort_v[i] = by_place[:, i * LANES : (i + 1) * LANES]
            sort_v[sort_rows + i] = goes_on[:, i * LANES : (i + 1) * LANES]
        target = iota((total, LANES), 1)
        up_to = jnp.sum(jnp.where(key_c <= target, 1, 0), axis=0, keepdims=True)
        at_it = jnp.sum(jnp.where(key_c == target, 1, 0), axis=0, keepdims=True)
        sort_v[2 * sort_rows] = jnp.where(at_it > 0, up_to, 0)

    def add_terms():
        run = jnp.zeros((vectors, size), f32)
        for i in range(sort_rows):
            count = min(LANES, term_count - i * LANES)

            def one(n, run):
                term = terms[sort_s[i, 0, n]].astype(f32)
                run = jnp.where(sort_s[sort_rows + i, 0, n] > 0, run + term, term)
                runs[i * LANES + n] = run
                return run

            run = lax.fori_loop(0, count, one, run, unroll=32)

    def total_of(b):
        last = sort_s[2 * sort_rows, 0, b]
        return jnp.where(last > 0, runs[jnp.maximum(last - 1, 0)], 0.0)

    def gram_rows(e):
        p = row_peer(e)
        return remote(
            gram.at[0], gram_row.at[my_row], gr_send.at[e], gr_recv.at[e], p, my_col
        )

    def gram_cols(d):
        q = col_peer(d)
        return remote(
            gram.at[1], gram_col.at[my_col], gc_send.at[d], gc_recv.at[d], my_row, q
        )

    me = my_row * n_col + my_col

    def gram_copy(e, d):
        at = e * n_col + d
        p, q = row_peer(e), col_peer(d)
        return remote(gram.at[2], gram_all.at[me], g_send.at[at], g_recv.at[at], p, q)

    def send_first(total):
        packed = pack_gram(total, vectors)
        gram[0] = packed
        for e in range(1, n_row):
            gram_rows(e).start()
        gram_row[my_row] = packed

    def pass_first():
        for e in range(1, n_row):
            gram_rows(e).wait()
        partial = jnp.sum(gram_row[...], axis=0)
        gram[1] = partial
        for d in reversed(range(1, n_col)):
            gram_cols(d).start()
        gram_col[my_col] = partial

    def take_first_sum():
        for d in range(1, n_col):
            gram_cols(d).wait()
        return jnp.sum(gram_col[...], axis=0) / order

    others = [(e, d) for e in range(n_row) for d in range(n_col) if e or d][::-1]

    def sum_second(total):
        packed = pack_gram(total, vectors)
        gram[2] = packed
        for e, d in others:
            gram_copy(e, d).start()
        gram_all[me] = packed
        for e, d in others:
            gram_copy(e, d).wait()
        return jnp.sum(gram_all[...], axis=0) / order

    no_gram = jnp.zeros((2 * vectors, 2 * vectors), f32)

    gather(True)
    sort_terms()
    copy_sort = pltpu.make_async_copy(sort_v, sort_s, own.at[4])
    copy_sort.start()
    load_blocks.wait()
    multiply()
    copy_sort.wait()
    wait_terms()
    add_terms()

    gather(False)

    def take_first(i, total):
        both = jnp.concatenate([total_of(2 * i), total_of(2 * i + 1)], axis=1)
        held[2 * i] = both[:, :size].astype(bf16)
        held[2 * i + 1] = both[:, size:].astype(bf16)
        return total + gram_term(both)

    total = lax.fori_loop(0, panel // 2, take_first, no_gram, unroll=16)
    send_first(total)
    multiply(pass_first)
    stack[...] = inverse_stack(factor_inverse(take_first_sum(), vectors))
    wait_terms()
    add_terms()
    stacked = stack[...]

    def take_second(i, total):
        both = jnp.concatenate([total_of(2 * i), total_of(2 * i + 1)], axis=1)
        both = apply_inverse(stacked, both)
        product[2 * i] = both[:, :size]
        product[2 * i + 1] = both[:, size:]
        return total + gram_term(both)

    total = lax.fori_loop(0, panel // 2, take_second, no_gram, unroll=32)
    inverse[...] = factor_inverse(sum_second(total), vectors)


def finish_kernel(chunks, source, inverse, out, done, sems):
    stacked = inverse_stack(inverse[...])
    pairs, wide = source.shape[0] // 2 // chunks, out.shape[1] // chunks

    def store(j):
        at = pl.ds(j * wide, wide)
        return pltpu.make_async_copy(done.at[:, at], out.at[:, at], sems.at[j])

    for j in range(chunks):
        for i in range(j * pairs, (j + 1) * pairs):
            done[:, i * 256 : (i + 1) * 256] = apply_inverse(stacked, pair(source, i))
        store(j).start()
    for j in range(chunks):
        store(j).wait()


def per_device(n_row, n_col, blocks, block_rows, block_cols, counts, start_vectors):
    slots, size = blocks.shape[0], blocks.shape[1]
    vectors, width = start_vectors.shape
    panel = width // size
    share = slots // n_col
    f32, bf16, i32 = jnp.float32, jnp.bfloat16, jnp.int32
    shape = jax.ShapeDtypeStruct
    dma = pltpu.SemaphoreType.DMA
    gram_shape = (8, vectors * vectors // 8)
    order = float(n_row * n_col * width)
    terms = slots * (n_row + 1)
    sort_shape = (2 * (-(-terms // LANES)) + 1, 1, LANES)
    by_owner = (n_col, share, vectors, size)
    slot_list = jnp.concatenate([block_rows, block_cols, counts], axis=1)
    product, inverse = pl.pallas_call(
        functools.partial(step_kernel, n_row, n_col, panel, order),
        out_shape=(shape((panel, vectors, size), f32), shape((vectors, vectors), f32)),
        in_specs=[VMEM, ANY, ANY],
        out_specs=(VMEM, VMEM),
        scratch_shapes=[
            pltpu.VMEM((vectors, width), f32),
            pltpu.VMEM((panel, vectors, size), bf16),
            pltpu.VMEM(blocks.shape, bf16),
            pltpu.VMEM(by_owner, bf16),
            pltpu.VMEM(by_owner, bf16),
            pltpu.VMEM(by_owner, bf16),
            pltpu.VMEM((n_row, slots, vectors, size), bf16),
            pltpu.VMEM((n_row, slots, vectors, size), bf16),
            pltpu.VMEM((terms, vectors, size), bf16),
            pltpu.VMEM((terms, vectors, size), f32),
            pltpu.VMEM((n_col, 1, LANES), i32),
            pltpu.VMEM((2, 1, LANES), i32),
            pltpu.VMEM((n_col, 1, LANES), i32),
            pltpu.VMEM((n_row, 1, LANES), i32),
            pltpu.VMEM(sort_shape, i32),
            pltpu.VMEM((vectors, 4 * vectors), bf16),
            pltpu.VMEM((3,) + gram_shape, f32),
            pltpu.VMEM((n_row,) + gram_shape, f32),
            pltpu.VMEM((n_col,) + gram_shape, f32),
            pltpu.VMEM((n_row * n_col,) + gram_shape, f32),
            pltpu.SMEM((2, 1, LANES), i32),
            pltpu.SMEM((n_col, 1, LANES), i32),
            pltpu.SMEM((n_row, 1, LANES), i32),
            pltpu.SMEM(sort_shape, i32),
            dma((5 + GROUPS,)),
            dma((n_col,)),
            dma((n_col,)),
            dma((n_row,)),
            dma((n_row,)),
            dma((n_col,)),
            dma((n_col,)),
            dma((n_col,)),
            dma((n_col,)),
            dma((n_row, GROUPS)),
            dma((n_row, GROUPS)),
            dma((n_row, GROUPS)),
            dma((n_row, GROUPS)),
            dma((n_row,)),
            dma((n_row,)),
            dma((n_col,)),
            dma((n_col,)),
            dma((n_row * n_col,)),
            dma((n_row * n_col,)),
        ],
        compiler_params=pltpu.CompilerParams(
            collective_id=1, has_side_effects=True, vmem_limit_bytes=KERNEL_BYTES
        ),
    )(slot_list, blocks, start_vectors)
    chunks = min(8, panel // 2)
    return pl.pallas_call(
        functools.partial(finish_kernel, chunks),
        out_shape=shape((vectors, width), f32),
        in_specs=[VMEM, VMEM],
        out_specs=ANY,
        scratch_shapes=[pltpu.VMEM((vectors, width), f32), dma((chunks,))],
        compiler_params=pltpu.CompilerParams(vmem_limit_bytes=KERNEL_BYTES),
    )(product, inverse)


def solution(mesh):
    placed = (
        P("row", "col", None),
        P("row", "col"),
        P("row", "col"),
        P("row", "col"),
        P(None, ("row", "col")),
    )
    return jax.shard_map(
        functools.partial(per_device, mesh.shape["row"], mesh.shape["col"]),
        mesh=mesh,
        in_specs=placed,
        out_specs=P(None, ("row", "col")),
        check_vma=False,
    )
```

```python
import functools

import jax
import jax.numpy as jnp
from jax import lax
from jax.experimental import pallas as pl
from jax.experimental.pallas import tpu as pltpu
from jax.sharding import PartitionSpec as P

ITERS = 2
GROUPS = 4
ORDER = (3, 1, 2, 0)
LANES = 128
MESH = pl.DeviceIdType.MESH
ANY = pl.BlockSpec(memory_space=pl.ANY)
VMEM = pl.BlockSpec(memory_space=pltpu.VMEM)
KERNEL_BYTES = 50 << 20
NO_KEY = 1 << 20


def partner(me, d, size):
    other, w = 0, 1
    while w < size:
        step = d // w if isinstance(d, int) else lax.div(d, w)
        other = other + w * lax.rem(lax.div(me, w) + step, 2)
        w *= 2
    return other


def split(value):
    high = value.astype(jnp.bfloat16)
    return high, (value - high.astype(jnp.float32)).astype(jnp.bfloat16)


def inverse_stack(inverse):
    high, low = split(inverse)
    return jnp.concatenate([high, low, high, low], axis=1)


def pair(blocks, i):
    return jnp.concatenate([blocks[2 * i], blocks[2 * i + 1]], axis=1)


def apply_inverse(stacked, product):
    high, low = split(product)
    parts = jnp.concatenate([high, high, low, low], axis=0)
    return jnp.dot(stacked, parts, preferred_element_type=jnp.float32)


def factor_inverse(packed, size):
    full = jnp.concatenate([packed[:, size * i : size * (i + 1)] for i in range(size // 8)], axis=0)
    rows = lax.broadcasted_iota(jnp.int32, (size, size), 0)
    lanes = lax.broadcasted_iota(jnp.int32, (size, size), 1)
    work = jnp.concatenate([full, (rows == lanes).astype(jnp.float32)], axis=1)
    row_ids = lax.broadcasted_iota(jnp.int32, work.shape, 0)
    for j in range(0, size, 8):
        columns = [jnp.broadcast_to(work[:, j + k : j + k + 1], work.shape) for k in range(8)]
        pivot_rows = [work[j + k : j + k + 1, :] for k in range(8)]
        for k in range(8):
            at = j + k
            scale = 1.0 / columns[k][at : at + 1, :]
            pivot_row = pivot_rows[k] * scale
            for m in range(k + 1, 8):
                factor = columns[m][at : at + 1, :] * scale
                pivot_rows[m] = pivot_rows[m] - columns[k][j + m : j + m + 1, :] * pivot_row
                columns[m] = columns[m] - columns[k] * factor
            work = work - jnp.where(row_ids > at, columns[k], 0.0) * pivot_row
    pivots = jnp.sum(jnp.where(rows == lanes, work[:, :size], 0.0), axis=1, keepdims=True)
    return work[:, size:] * (1.0 / jnp.sqrt(pivots))


def gram_term(value):
    high, low = split(value)
    parts = jnp.concatenate([high, low], axis=0)
    return lax.dot_general(
        parts, parts, (((1,), (1,)), ((), ())), preferred_element_type=jnp.float32
    )


def pack_gram(total, vectors):
    upper = total[:vectors] + total[vectors:]
    full = upper[:, :vectors] + upper[:, vectors:]
    return jnp.concatenate([full[8 * i : 8 * i + 8] for i in range(vectors // 8)], axis=1)


def iota(shape, axis):
    return lax.broadcasted_iota(jnp.int32, shape, axis)


def column(row):
    n = row.shape[1]
    return jnp.sum(jnp.where(iota((n, n), 0) == iota((n, n), 1), row, 0), axis=1, keepdims=True)


def step_kernel(
    n_row,
    n_col,
    panel,
    order,
    slot_list,
    blocks,
    source,
    product,
    inverse,
    source_in,
    held,
    held_blocks,
    c_out,
    c_in,
    c_back,
    r_out,
    r_in,
    terms,
    runs,
    ask,
    mine,
    lists_v,
    asked_v,
    sort_v,
    stack,
    gram,
    gram_row,
    gram_col,
    gram_all,
    mine_s,
    lists,
    asked,
    sort_s,
    own,
    l_send,
    l_recv,
    a_send,
    a_recv,
    c_send,
    c_recv,
    cb_send,
    cb_recv,
    r_send,
    r_recv,
    rb_send,
    rb_recv,
    gr_send,
    gr_recv,
    gc_send,
    gc_recv,
    g_send,
    g_recv,
):
    slots, size = held_blocks.shape[0], held_blocks.shape[1]
    vectors = held.shape[1]
    share = slots // n_col
    per = n_col // GROUPS
    piece = per * share
    my_row, my_col = lax.axis_index("row"), lax.axis_index("col")
    base = my_row * panel
    f32, bf16 = jnp.float32, jnp.bfloat16

    load_source = pltpu.make_async_copy(source, source_in, own.at[0])
    load_blocks = pltpu.make_async_copy(blocks, held_blocks, own.at[1])

    def col_peer(d):
        return partner(my_col, d, n_col)

    def row_peer(e):
        return partner(my_row, e, n_row)

    def remote(src, dst, send, recv, row, col):
        return pltpu.make_async_remote_copy(
            src_ref=src,
            dst_ref=dst,
            send_sem=send,
            recv_sem=recv,
            device_id=(row, col),
            device_id_type=MESH,
        )

    barrier = pltpu.get_barrier_semaphore()
    for d in range(1, n_col):
        pl.semaphore_signal(barrier, inc=1, device_id=(my_row, col_peer(d)), device_id_type=MESH)
    for e in range(1, n_row):
        pl.semaphore_signal(barrier, inc=1, device_id=(row_peer(e), my_col), device_id_type=MESH)

    load_source.start()
    load_blocks.start()
    rows, cols = slot_list[:, :slots], slot_list[:, slots : 2 * slots]

    shift = panel.bit_length() - 1
    owner = lax.shift_right_logical(rows, shift)
    owner_c = column(owner)
    before = iota((slots, slots), 0) < iota((slots, slots), 1)
    rank = jnp.sum(jnp.where((owner_c == owner) & before, 1, 0), axis=0, keepdims=True)
    rank_c = column(rank)
    place_c = owner_c * share + rank_c
    ids = iota((slots, 1), 0)
    live = ids < slot_list[:, 2 * slots : 2 * slots + 1]
    row_c = jnp.where(live, column(rows & (panel - 1)) + 1, 0)
    col_c = jnp.where(live, column(cols) + 1, 0)
    lanes = iota((slots, LANES), 1)
    here = place_c == lanes
    mine[0] = jnp.sum(jnp.where(here, ids, 0), axis=0, keepdims=True)
    mine[1] = jnp.sum(jnp.where(here, col_c, 0), axis=0, keepdims=True)
    mine_place = rank_c == lanes - my_col * share
    for o in range(n_col):
        ask[o] = jnp.sum(
            jnp.where(mine_place & (owner_c == o), row_c, 0), axis=0, keepdims=True
        )
    take_mine = pltpu.make_async_copy(mine, mine_s, own.at[2])
    take_mine.start()
    lists_v[my_col] = ask[my_col]
    asked_v[my_row] = mine[1]

    load_source.wait()
    for b in range(panel):
        held[b] = source_in[:, b * size : (b + 1) * size].astype(bf16)

    pl.semaphore_wait(barrier, n_col + n_row - 2)

    def row_ask(e):
        p = row_peer(e)
        return remote(
            mine.at[1], asked_v.at[my_row], a_send.at[e], a_recv.at[e], p, my_col
        )

    def col_ask(d):
        q = col_peer(d)
        return remote(
            ask.at[q], lists_v.at[my_col], l_send.at[d], l_recv.at[d], my_row, q
        )

    def first_peer(g):
        return partner(lax.div(my_col, per), g, GROUPS) * per

    def take_lists(g):
        at = pl.ds(first_peer(g), per)
        return pltpu.make_async_copy(lists_v.at[at], lists.at[at], own.at[5 + g])

    take_asked = pltpu.make_async_copy(asked_v, asked, own.at[4])
    for e in range(1, n_row):
        row_ask(e).start()
    for d in reversed(range(1, n_col)):
        col_ask(d).start()
    take_mine.wait()
    for e in range(1, n_row):
        row_ask(e).wait()
    take_asked.start()
    take_asked.wait()

    def first_slot(g):
        return first_peer(g) * share

    def row_copy(g, e):
        at = pl.ds(first_slot(g), piece)
        p = row_peer(e)
        return remote(
            r_out.at[e, at], r_in.at[e, at], r_send.at[e, g], r_recv.at[e, g], p, my_col
        )

    def row_back(g, e):
        at = pl.ds(slots + my_row * slots + first_slot(g), piece)
        p = row_peer(e)
        return remote(
            terms.at[at], terms.at[at], rb_send.at[e, g], rb_recv.at[e, g], p, my_col
        )

    def col_copy(d):
        return remote(
            c_out.at[d], c_in.at[d], c_send.at[d], c_recv.at[d], my_row, col_peer(d)
        )

    def col_back(d):
        at = pl.ds(my_col * share, share)
        return remote(
            c_back.at[d], terms.at[at], cb_send.at[d], cb_recv.at[d], my_row, col_peer(d)
        )

    def gather(first):
        def block(at):
            if first:
                return held[at]
            return total_of(at).astype(bf16)

        def gather_rows(g):
            for e in range(1, n_row):
                p, start = row_peer(e), first_slot(g)

                def one_r(n, carry):
                    at = asked[p, 0, start + n] - 1 - base
                    r_out[e, start + n] = block(jnp.clip(at, 0, panel - 1))
                    return carry

                lax.fori_loop(0, piece, one_r, 0, unroll=8)
                row_copy(g, e).start()

        def gather_cols(g):
            if first:
                for d in reversed(range(max(g * per, 1), (g + 1) * per)):
                    col_ask(d).wait()
                take_lists(g).start()
                take_lists(g).wait()

            def one_c(i, carry):
                d = (g + 1) * per - 1 - i
                q = col_peer(d)
                for a in range(share):
                    at = jnp.maximum(lists[q, 0, q * share + a] - 1, 0)
                    c_out[d, a] = block(at)
                col_copy(d).start()
                return carry

            lax.fori_loop(0, per if g else per - 1, one_c, 0)

        for g in ORDER:
            gather_rows(g)
            gather_cols(g)
        for a in range(share):
            at = jnp.maximum(lists[my_col, 0, my_col * share + a] - 1, 0)
            c_in[0, a] = block(at)

    def multiply(between=None):
        for g in ORDER:
            if between is not None and g == ORDER[1]:
                between()
            for e in range(1, n_row):
                row_copy(g, e).wait()

            def one_peer(i, own_terms=False):
                d = (g + 1) * per - 1 - i
                q = my_col if own_terms else col_peer(d)
                for a in range(share):
                    t = q * share + a
                    block = held_blocks[mine_s[0, 0, t]]
                    col = mine_s[1, 0, t] - 1
                    x_col = held[jnp.clip(col - base, 0, panel - 1)]
                    for e in range(1, n_row):
                        first_col = row_peer(e) * panel
                        there = (col >= first_col) & (col < first_col + panel)
                        x_col = jnp.where(there, r_in[e, t], x_col)
                    row_product = lax.dot_general(
                        x_col, block, (((1,), (1,)), ((), ())), preferred_element_type=f32
                    )
                    col_product = jnp.dot(c_in[d, a], block, preferred_element_type=f32)
                    if own_terms:
                        terms[t] = row_product.astype(bf16)
                    else:
                        c_back[d, a] = row_product.astype(bf16)
                    terms[slots + my_row * slots + t] = col_product.astype(bf16)

            peers = per if g else per - 1
            for i in range(peers):
                col_copy((g + 1) * per - 1 - i).wait()
            for i in range(per):
                one_peer(i, own_terms=i == peers)
            for i in range(peers):
                col_back((g + 1) * per - 1 - i).start()
            for e in range(1, n_row):
                row_back(g, e).start()

    def wait_terms():
        for g in ORDER:
            for e in range(1, n_row):
                row_back(g, e).wait()

        def one(i, carry):
            col_back(n_col - 1 - i).wait()
            return carry

        lax.fori_loop(0, n_col - 1, one, 0)

    term_count = slots * (n_row + 1)
    sort_rows = -(-term_count // LANES)

    def sort_terms():
        key_parts = []
        found = jnp.sum(lists_v[...], axis=0)
        key_parts.append(jnp.where(found > 0, found - 1, NO_KEY)[:, :slots])
        for p in range(n_row):
            at = asked_v[p] - 1 - base
            key_parts.append(jnp.where((at >= 0) & (at < panel), at, NO_KEY)[:, :slots])
        tail = sort_rows * LANES - term_count
        if tail:
            key_parts.append(jnp.full((1, tail), NO_KEY, jnp.int32))
        key = jnp.concatenate(key_parts, axis=1)
        total = sort_rows * LANES
        key_c = column(key)
        ids_c, ids_r = iota((total, total), 0), iota((total, total), 1)
        twin = (key_c == key) & (ids_c < ids_r)
        rank = jnp.sum(jnp.where(twin | (key_c < key), 1, 0), axis=0, keepdims=True)
        again = jnp.sum(jnp.where(twin, 1, 0), axis=0, keepdims=True)
        here = column(rank) == ids_r
        by_place = jnp.sum(jnp.where(here, ids_c, 0), axis=0, keepdims=True)
        goes_on = jnp.sum(jnp.where(here, column(again), 0), axis=0, keepdims=True)
        for i in range(sort_rows):
            sort_v[i] = by_place[:, i * LANES : (i + 1) * LANES]
            sort_v[sort_rows + i] = goes_on[:, i * LANES : (i + 1) * LANES]
        target = iota((total, LANES), 1)
        up_to = jnp.sum(jnp.where(key_c <= target, 1, 0), axis=0, keepdims=True)
        at_it = jnp.sum(jnp.where(key_c == target, 1, 0), axis=0, keepdims=True)
        sort_v[2 * sort_rows] = jnp.where(at_it > 0, up_to, 0)

    def add_terms():
        run = jnp.zeros((vectors, size), f32)
        for i in range(sort_rows):
            count = min(LANES, term_count - i * LANES)

            def one(n, run):
                term = terms[sort_s[i, 0, n]].astype(f32)
                run = jnp.where(sort_s[sort_rows + i, 0, n] > 0, run + term, term)
                runs[i * LANES + n] = run
                return run

            run = lax.fori_loop(0, count, one, run, unroll=64)

    def total_of(b):
        last = sort_s[2 * sort_rows, 0, b]
        return jnp.where(last > 0, runs[jnp.maximum(last - 1, 0)], 0.0)

    def gram_rows(e):
        p = row_peer(e)
        return remote(
            gram.at[0], gram_row.at[my_row], gr_send.at[e], gr_recv.at[e], p, my_col
        )

    def gram_cols(d):
        q = col_peer(d)
        return remote(
            gram.at[1], gram_col.at[my_col], gc_send.at[d], gc_recv.at[d], my_row, q
        )

    me = my_row * n_col + my_col

    def gram_copy(e, d):
        at = e * n_col + d
        p, q = row_peer(e), col_peer(d)
        return remote(gram.at[2], gram_all.at[me], g_send.at[at], g_recv.at[at], p, q)

    def send_first(total):
        packed = pack_gram(total, vectors)
        gram[0] = packed
        for e in range(1, n_row):
            gram_rows(e).start()
        gram_row[my_row] = packed

    def pass_first():
        for e in range(1, n_row):
            gram_rows(e).wait()
        partial = jnp.sum(gram_row[...], axis=0)
        gram[1] = partial
        for d in reversed(range(1, n_col)):
            gram_cols(d).start()
        gram_col[my_col] = partial

    def take_first_sum():
        for d in range(1, n_col):
            gram_cols(d).wait()
        return jnp.sum(gram_col[...], axis=0) / order

    others = [(e, d) for e in range(n_row) for d in range(n_col) if e or d][::-1]

    def sum_second(total):
        packed = pack_gram(total, vectors)
        gram[2] = packed
        for e, d in others:
            gram_copy(e, d).start()
        gram_all[me] = packed
        for e, d in others:
            gram_copy(e, d).wait()
        return jnp.sum(gram_all[...], axis=0) / order

    no_gram = jnp.zeros((2 * vectors, 2 * vectors), f32)

    gather(True)
    sort_terms()
    copy_sort = pltpu.make_async_copy(sort_v, sort_s, own.at[4])
    copy_sort.start()
    load_blocks.wait()
    multiply()
    copy_sort.wait()
    wait_terms()
    add_terms()

    gather(False)

    def take_first(i, total):
        both = jnp.concatenate([total_of(2 * i), total_of(2 * i + 1)], axis=1)
        held[2 * i] = both[:, :size].astype(bf16)
        held[2 * i + 1] = both[:, size:].astype(bf16)
        return total + gram_term(both)

    total = lax.fori_loop(0, panel // 2, take_first, no_gram, unroll=16)
    send_first(total)
    multiply(pass_first)
    stack[...] = inverse_stack(factor_inverse(take_first_sum(), vectors))
    wait_terms()
    add_terms()
    stacked = stack[...]

    def take_second(i, total):
        both = jnp.concatenate([total_of(2 * i), total_of(2 * i + 1)], axis=1)
        both = apply_inverse(stacked, both)
        product[2 * i] = both[:, :size]
        product[2 * i + 1] = both[:, size:]
        return total + gram_term(both)

    total = lax.fori_loop(0, panel // 2, take_second, no_gram, unroll=True)
    inverse[...] = factor_inverse(sum_second(total), vectors)


def finish_kernel(chunks, source, inverse, out, done, sems):
    stacked = inverse_stack(inverse[...])
    pairs, wide = source.shape[0] // 2 // chunks, out.shape[1] // chunks

    def store(j):
        at = pl.ds(j * wide, wide)
        return pltpu.make_async_copy(done.at[:, at], out.at[:, at], sems.at[j])

    for j in range(chunks):
        for i in range(j * pairs, (j + 1) * pairs):
            done[:, i * 256 : (i + 1) * 256] = apply_inverse(stacked, pair(source, i))
        store(j).start()
    for j in range(chunks):
        store(j).wait()


def per_device(n_row, n_col, blocks, block_rows, block_cols, counts, start_vectors):
    slots, size = blocks.shape[0], blocks.shape[1]
    vectors, width = start_vectors.shape
    panel = width // size
    share = slots // n_col
    f32, bf16, i32 = jnp.float32, jnp.bfloat16, jnp.int32
    shape = jax.ShapeDtypeStruct
    dma = pltpu.SemaphoreType.DMA
    gram_shape = (8, vectors * vectors // 8)
    order = float(n_row * n_col * width)
    terms = slots * (n_row + 1)
    sort_shape = (2 * (-(-terms // LANES)) + 1, 1, LANES)
    by_owner = (n_col, share, vectors, size)
    slot_list = jnp.concatenate([block_rows, block_cols, counts], axis=1)
    product, inverse = pl.pallas_call(
        functools.partial(step_kernel, n_row, n_col, panel, order),
        out_shape=(shape((panel, vectors, size), f32), shape((vectors, vectors), f32)),
        in_specs=[VMEM, ANY, ANY],
        out_specs=(VMEM, VMEM),
        scratch_shapes=[
            pltpu.VMEM((vectors, width), f32),
            pltpu.VMEM((panel, vectors, size), bf16),
            pltpu.VMEM(blocks.shape, bf16),
            pltpu.VMEM(by_owner, bf16),
            pltpu.VMEM(by_owner, bf16),
            pltpu.VMEM(by_owner, bf16),
            pltpu.VMEM((n_row, slots, vectors, size), bf16),
            pltpu.VMEM((n_row, slots, vectors, size), bf16),
            pltpu.VMEM((terms, vectors, size), bf16),
            pltpu.VMEM((terms, vectors, size), f32),
            pltpu.VMEM((n_col, 1, LANES), i32),
            pltpu.VMEM((2, 1, LANES), i32),
            pltpu.VMEM((n_col, 1, LANES), i32),
            pltpu.VMEM((n_row, 1, LANES), i32),
            pltpu.VMEM(sort_shape, i32),
            pltpu.VMEM((vectors, 4 * vectors), bf16),
            pltpu.VMEM((3,) + gram_shape, f32),
            pltpu.VMEM((n_row,) + gram_shape, f32),
            pltpu.VMEM((n_col,) + gram_shape, f32),
            pltpu.VMEM((n_row * n_col,) + gram_shape, f32),
            pltpu.SMEM((2, 1, LANES), i32),
            pltpu.SMEM((n_col, 1, LANES), i32),
            pltpu.SMEM((n_row, 1, LANES), i32),
            pltpu.SMEM(sort_shape, i32),
            dma((5 + GROUPS,)),
            dma((n_col,)),
            dma((n_col,)),
            dma((n_row,)),
            dma((n_row,)),
            dma((n_col,)),
            dma((n_col,)),
            dma((n_col,)),
            dma((n_col,)),
            dma((n_row, GROUPS)),
            dma((n_row, GROUPS)),
            dma((n_row, GROUPS)),
            dma((n_row, GROUPS)),
            dma((n_row,)),
            dma((n_row,)),
            dma((n_col,)),
            dma((n_col,)),
            dma((n_row * n_col,)),
            dma((n_row * n_col,)),
        ],
        compiler_params=pltpu.CompilerParams(
            collective_id=1, has_side_effects=True, vmem_limit_bytes=KERNEL_BYTES
        ),
    )(slot_list, blocks, start_vectors)
    chunks = min(8, panel // 2)
    return pl.pallas_call(
        functools.partial(finish_kernel, chunks),
        out_shape=shape((vectors, width), f32),
        in_specs=[VMEM, VMEM],
        out_specs=ANY,
        scratch_shapes=[pltpu.VMEM((vectors, width), f32), dma((chunks,))],
        compiler_params=pltpu.CompilerParams(vmem_limit_bytes=KERNEL_BYTES),
    )(product, inverse)


def solution(mesh):
    placed = (
        P("row", "col", None),
        P("row", "col"),
        P("row", "col"),
        P("row", "col"),
        P(None, ("row", "col")),
    )
    return jax.shard_map(
        functools.partial(per_device, mesh.shape["row"], mesh.shape["col"]),
        mesh=mesh,
        in_specs=placed,
        out_specs=P(None, ("row", "col")),
        check_vma=False,
    )
```
